32 devices in a mesh: batch: 8 (over y, x, core), tensor: 4 (over z).
Axes of the slice: x: 2, y: 2, z: 4, core: 2. Of those that a mesh axis runs over, the one named last changes fastest.
Arguments:
- images: bfloat16 [192, 196, 768], P('batch'), may hold values from -6 to 6
- counts: int32 [8], P('batch'), may hold values from 6 to 24, as said below
- ln1_gain: float32 [768], replicated, may hold values from 0.1 to 1.9
- ln1_bias: float32 [768], replicated, may hold values from -1.5 to 1.5
- tok_w1: bfloat16 [196, 384], replicated, may hold values from -0.4375 to 0.4375
- tok_b1: float32 [384], replicated, may hold values from -1.5 to 1.5
- tok_w2: bfloat16 [384, 196], replicated, may hold values from -0.3125 to 0.3125
- tok_b2: float32 [196], replicated, may hold values from -1.5 to 1.5
- ln2_gain: float32 [768], replicated, may hold values from 0.1 to 1.9
- ln2_bias: float32 [768], replicated, may hold values from -1.5 to 1.5
- chan_w1: bfloat16 [768, 3072], P(None, 'tensor'), may hold values from -0.21875 to 0.21875
- chan_b1: float32 [3072], P('tensor'), may hold values from -1.5 to 1.5
- chan_w2: bfloat16 [3072, 768], P('tensor'), may hold values from -0.109375 to 0.109375
- chan_b2: float32 [768], replicated, may hold values from -1.5 to 1.5
- cotangent: bfloat16 [192, 196, 768], P('batch'), may hold values from -6 to 6
Outputs:
- output: bfloat16 [192, 196, 768], P(('batch', 'tensor'))
- grad_images: float32 [192, 196, 768], P(('batch', 'tensor'))
- grad_ln1_gain: float32 [768], replicated
- grad_ln1_bias: float32 [768], replicated
- grad_tok_w1: float32 [196, 384], replicated
- grad_tok_b1: float32 [384], replicated
- grad_tok_w2: float32 [384, 196], replicated
- grad_tok_b2: float32 [196], replicated
- grad_ln2_gain: float32 [768], replicated
- grad_ln2_bias: float32 [768], replicated
- grad_chan_w1: float32 [768, 3072], P(None, 'tensor')
- grad_chan_b1: float32 [3072], P('tensor')
- grad_chan_w2: float32 [3072, 768], P('tensor')
- grad_chan_b2: float32 [768], replicated
The draws below stay inside these ranges and needn't reach their ends.
Inputs may be any that keep to these rules, and one draw needn't show every extreme that they name: Batch index b holds images in its first counts[b] slots; the others are padding. Some index is full and some holds the fewest in every draw.
All inputs are finite; a program needn't handle non-finite values.
Results may differ from the reference program's by a relative error of at most 0.0068.
Values may be sent and summed in bfloat16 or wider, within the bound.
A program may use at most 320 MiB of HBM per device.

```python
import jax
import jax.numpy as jnp
from jax import lax

D = 768
S = 196
DS = 384
DC = 3072
IMG_DEV = 24
IMAGES = 192
N_BATCH = 8


def draw_counts(key, part):
    first_key, second_key, third_key = jax.random.split(key, 3)
    base = jax.random.randint(first_key, (N_BATCH,), IMG_DEV // 4, IMG_DEV + 1, dtype=jnp.int32)
    full_spot = jax.random.randint(second_key, (), 0, N_BATCH, dtype=jnp.int32)
    offset = jax.random.randint(third_key, (), 1, N_BATCH, dtype=jnp.int32)
    low_spot = (full_spot + offset) % N_BATCH
    base = base.at[full_spot].set(IMG_DEV)
    return base.at[low_spot].set(IMG_DEV // 4)


def block_levels(own_key, shape, cuts, smallest, high):
    def one(axis_at, shards_of):
        steps = jax.random.uniform(jax.random.fold_in(jax.random.fold_in(own_key, 6), axis_at), (shards_of,), jnp.float32, smallest / len(cuts), high / len(cuts))
        return jnp.repeat(jnp.exp(steps), shape[axis_at] // shards_of).reshape((-1,) + (1,) * (len(shape) - axis_at - 1))

    level = one(*cuts[0])
    for cut in cuts[1:]:
        level = level * one(*cut)
    return level


def gaussian(key, dims, scale, limit, shards=(), held_as=jnp.bfloat16):
    drawn = scale * jax.random.normal(key, dims, jnp.float32)
    if shards:
        drawn = drawn * block_levels(key, dims, shards, -0.22, 0.18)
    return jnp.clip(drawn, -limit, limit).astype(held_as)


def setup_inputs(seed: int = 0) -> dict:
    splits = jax.random.split(jax.random.key(seed), 16)
    images = gaussian(splits[0], (IMAGES, S, D), 1.0, 6.0, ((0, 8),))
    counts = draw_counts(jax.random.fold_in(splits[15], 71), 0)
    ln1_gain = jnp.clip(1.0 + 0.18 * jax.random.normal(splits[2], (D,), jnp.float32), 0.1, 1.9)
    ln1_bias = gaussian(splits[3], (D,), 0.3, 1.5, (), jnp.float32)
    tok_w1 = gaussian(splits[4], (S, DS), S ** -0.5, 0.4375)
    tok_b1 = gaussian(splits[5], (DS,), 0.3, 1.5, (), jnp.float32)
    tok_w2 = gaussian(splits[6], (DS, S), DS ** -0.5, 0.3125)
    tok_b2 = gaussian(splits[7], (S,), 0.3, 1.5, (), jnp.float32)
    ln2_gain = jnp.clip(1.0 + 0.18 * jax.random.normal(splits[8], (D,), jnp.float32), 0.1, 1.9)
    ln2_bias = gaussian(splits[9], (D,), 0.3, 1.5, (), jnp.float32)
    chan_w1 = gaussian(splits[10], (D, DC), D ** -0.5, 0.21875, ((1, 4),))
    chan_b1 = gaussian(splits[11], (DC,), 0.3, 1.5, ((0, 4),), jnp.float32)
    chan_w2 = gaussian(splits[12], (DC, D), DC ** -0.5, 0.109375, ((0, 4),))
    chan_b2 = gaussian(splits[13], (D,), 0.3, 1.5, (), jnp.float32)
    cotangent = gaussian(splits[14], (IMAGES, S, D), 1.0, 6.0, ((0, 8),))
    return dict(images=images, counts=counts, ln1_gain=ln1_gain, ln1_bias=ln1_bias, tok_w1=tok_w1, tok_b1=tok_b1, tok_w2=tok_w2, tok_b2=tok_b2, ln2_gain=ln2_gain, ln2_bias=ln2_bias, chan_w1=chan_w1, chan_b1=chan_b1, chan_w2=chan_w2, chan_b2=chan_b2, cotangent=cotangent)


@jax.custom_vjp
def low(v):
    return lax.optimization_barrier(v.astype(jnp.bfloat16)).astype(jnp.float32)

@jax.custom_vjp
def low_back(v):
    return v

def low_keep(v):
    return (low(v), None)

def low_pass(kept, grad):
    return (grad,)

def back_keep(v):
    return (v, None)

def back_low(kept, grad):
    return (low(grad),)
low.defvjp(low_keep, low_pass)
low_back.defvjp(back_keep, back_low)
EPSILON = 1e-06
HIGH = lax.Precision.HIGHEST

def layer_norm(values, gain, bias):
    center = values - lax.optimization_barrier(jnp.mean(values, axis=-1, keepdims=True))
    scaled = center * lax.rsqrt(lax.optimization_barrier(jnp.mean(center * center, axis=-1, keepdims=True)) + EPSILON)
    return scaled * gain + bias

def forward(params, inputs):
    gain_one, bias_one, tok_w1, tok_b1, tok_w2, tok_b2, gain_two, bias_two, chan_w1, chan_b1, chan_w2, chan_b2 = params
    normed_one = low(layer_norm(inputs, gain_one, bias_one))
    tok_hidden = jnp.einsum('ipd,pk->ikd', normed_one, tok_w1, precision=HIGH) + tok_b1[None, :, None]
    tok_hidden = low_back(tok_hidden)
    tok_act = low(jax.nn.gelu(tok_hidden, approximate=False))
    mixed = jnp.einsum('ikd,kp->ipd', tok_act, tok_w2, precision=HIGH) + tok_b2[None, :, None]
    mixed = inputs + low_back(mixed)
    normed_two = low(layer_norm(mixed, gain_two, bias_two))
    chan_hidden = low_back(jnp.einsum('isd,dk->isk', normed_two, chan_w1, precision=HIGH) + chan_b1)
    chan_act = low(jax.nn.gelu(chan_hidden, approximate=False))
    return mixed + jnp.einsum('isk,kd->isd', chan_act, chan_w2, precision=HIGH) + chan_b2

def reference(images, counts, ln1_gain, ln1_bias, tok_w1, tok_b1, tok_w2, tok_b2, ln2_gain, ln2_bias, chan_w1, chan_b1, chan_w2, chan_b2, cotangent):
    params = tuple((item.astype(jnp.float32) for item in (ln1_gain, ln1_bias, tok_w1, tok_b1, tok_w2, tok_b2, ln2_gain, ln2_bias, chan_w1, chan_b1, chan_w2, chan_b2)))
    blocks = images.reshape(N_BATCH, IMG_DEV, S, D)
    cot_blocks = cotangent.reshape(N_BATCH, IMG_DEV, S, D)

    def step(carry, item):
        block, cot_block, count = item
        valid = (jnp.arange(IMG_DEV, dtype=jnp.int32) < count).astype(jnp.float32)
        result, pullback = jax.vjp(forward, params, block.astype(jnp.float32))
        grads, grad_in = pullback(cot_block.astype(jnp.float32) * valid[:, None, None])
        carry = jax.tree.map(lambda total, extra: total + extra, carry, grads)
        return (carry, (result.astype(jnp.bfloat16), grad_in))
    zeros = jax.tree.map(jnp.zeros_like, params)
    totals, (results, grads_in) = lax.scan(step, zeros, (blocks, cot_blocks, counts))
    return (results.reshape(IMAGES, S, D), grads_in.reshape(IMAGES, S, D), totals[0], totals[1], totals[2], totals[3], totals[4], totals[5], totals[6], totals[7], totals[8], totals[9], totals[10], totals[11])
```

```python
import jax
import jax.numpy as jnp
from jax import lax
from jax.experimental import pallas as pl
from jax.experimental.pallas import tpu as pltpu
from jax.sharding import PartitionSpec as P

EPSILON = 1e-06
ROOT_HALF = 0.7071067811865476
INV_ROOT_TAU = 0.3989422804014327
MESH = pl.DeviceIdType.MESH
BF = jnp.bfloat16
F32 = jnp.float32
RING = 8


def dot(a, b):
    return lax.dot_general(a, b, (((1,), (0,)), ((), ())), preferred_element_type=F32)


def dot_nt(a, b):
    return lax.dot_general(a, b, (((1,), (1,)), ((), ())), preferred_element_type=F32)


def dot_tn(a, b):
    return lax.dot_general(a, b, (((0,), (0,)), ((), ())), preferred_element_type=F32)


def flip(v, bit):
    step = 1 << bit
    return v + (1 - 2 * ((v // step) % 2)) * step


def normal(v):
    center = v - jnp.mean(v, axis=-1, keepdims=True)
    inverse = lax.rsqrt(jnp.mean(center * center, axis=-1, keepdims=True) + EPSILON)
    return center * inverse, inverse


def cdf(v):
    return 0.5 * (1.0 + lax.erf(v * ROOT_HALF))


def slope(v, p):
    return p + v * jnp.exp(-0.5 * v * v) * INV_ROOT_TAU


def norm_back(grad, gain, scaled, inverse):
    weighted = grad * gain
    return inverse * (
        weighted
        - jnp.mean(weighted, axis=-1, keepdims=True)
        - scaled * jnp.mean(weighted * scaled, axis=-1, keepdims=True)
    )


def eye(n, dtype):
    rows = lax.broadcasted_iota(jnp.int32, (n, n), 0)
    cols = lax.broadcasted_iota(jnp.int32, (n, n), 1)
    return jnp.where(rows == cols, 1.0, 0.0).astype(dtype)


def column(row):
    n = row.shape[1]
    return jnp.sum(eye(n, F32) * row, axis=1, keepdims=True)


def per_device(nb, nt, args):
    (images, counts, g1, b1, tw1, tb1, tw2, tb2, g2, b2, cw1, cb1, cw2, cb2, cot) = args
    slots, S, D = images.shape
    DS = tw1.shape[1]
    H = cw1.shape[1]
    own = slots // nt
    SP = -(-S // 16) * 16
    pairs = own // 2
    rows = own * SP
    chunk = 2 * SP
    n_chunk = rows // chunk
    piece = D // RING
    SM = 512
    HD = D // 2

    def kernel(
        img, cot_h, w1_h, w2_h, cb1_r, cnt, g1_r, b1_r, g2_r, b2_r, tw1_r, tw2_r, tb1_r, tb2_r, cb2_r,
        out_h, gim_h, gw1_r, gw2_r, sm_r,
        W1, W2, B1, xb, gb, n2, gp, ca, dch, dacc, u_s, ta_s, n1_s, w1t, w2t, tb1c, tb2c, gcb1, vec, tb2acc, ob, gi,
        x_sem, g_sem, l_sem, o_sem, i_sem, zs, zr, ps, pr, bs, br,
    ):
        b = lax.axis_index("batch")
        t = lax.axis_index("tensor")
        l = b % RING
        base = b - l
        c = l % 2
        lf, ls = flip(l, 1), flip(l, 2)
        p_first = (1 - c) * lf + c * ls
        p_second = (1 - c) * ls + c * lf
        p_both = flip(flip(l, 1), 2)
        p_core = flip(l, 0)
        zpeer = [(t + k) % nt for k in range(1, nt)]

        bar = pltpu.get_barrier_semaphore()
        partners = [(b, z) for z in zpeer] + [(base + v, t) for v in (p_first, p_second, p_core)]
        for d in partners:
            pl.semaphore_signal(bar, inc=1, device_id=d, device_id_type=MESH)

        def fetch(q, slot):
            grp = (t + 1 + q // pairs) % nt
            start = own * grp + 2 * (q % pairs)
            return (
                pltpu.make_async_copy(img.at[pl.ds(start, 2)], xb.at[slot], x_sem.at[slot]),
                pltpu.make_async_copy(cot_h.at[pl.ds(start, 2)], gb.at[slot], g_sem.at[slot]),
            )

        for cp in fetch(0, 0):
            cp.start()
        local = [
            pltpu.make_async_copy(w1_h, W1.at[t], l_sem.at[0]),
            pltpu.make_async_copy(w2_h, W2.at[t], l_sem.at[1]),
        ]
        for cp in local:
            cp.start()
        B1[t] = cb1_r[...]

        pl.semaphore_wait(bar, len(partners))

        mine = pl.ds(pl.multiple_of(l * piece, piece), piece)

        def z_copy(k, arr):
            src = (w1_h, w2_h)[arr].at[mine]
            dst = (W1, W2)[arr].at[t, mine]
            return pltpu.make_async_remote_copy(
                src, dst, zs.at[k, arr], zr.at[k, arr], device_id=(b, (t + k) % nt), device_id_type=MESH
            )

        def b_copy(k):
            return pltpu.make_async_remote_copy(
                cb1_r, B1.at[t], bs.at[k], br.at[k], device_id=(b, (t + k) % nt), device_id_type=MESH
            )

        for k in range(1, nt):
            for arr in range(2):
                z_copy(k, arr).start()
            b_copy(k).start()

        def plane(k, stage):
            shard = (t + nt - k) % nt
            first = (l,) if stage == 0 else (l, p_first) if stage == 1 else (l, p_first, p_second, p_both)
            peer = (p_first, p_second, p_core)[stage]
            at = (0, 1, 3)[stage]
            copies = []
            for j, who in enumerate(first):
                part = pl.ds(pl.multiple_of(who * piece, piece), piece)
                for arr in range(2):
                    ref = (W1, W2)[arr].at[shard, part]
                    copies.append(
                        pltpu.make_async_remote_copy(
                            ref, ref, ps.at[k, at + j, arr], pr.at[k, at + j, arr],
                            device_id=(base + peer, t), device_id_type=MESH,
                        )
                    )
            return copies

        def act(k, stage):
            if stage == 0:
                for arr in range(2):
                    z_copy(k, arr).wait()
                b_copy(k).wait()
            else:
                for cp in plane(k, stage - 1):
                    cp.wait()
            if stage < 3:
                for cp in plane(k, stage):
                    cp.start()

        w1t[...] = dot_nt(eye(DS, BF), tw1_r[...]).astype(BF)
        w2t[...] = dot_nt(eye(S, BF), tw2_r[...]).astype(BF)
        tb1c[...] = column(tb1_r[...])
        tb2c[...] = column(tb2_r[...])
        gw1_r[...] = jnp.zeros_like(gw1_r)
        gw2_r[...] = jnp.zeros_like(gw2_r)
        gcb1[...] = jnp.zeros_like(gcb1)
        vec[...] = jnp.zeros_like(vec)
        tb2acc[...] = jnp.zeros_like(tb2acc)
        sm_r[...] = jnp.zeros_like(sm_r)
        pad = SP - S
        for i in range(own):
            n2[i * SP + S : (i + 1) * SP, :] = jnp.zeros((pad, D), BF)
            gp[i * SP + S : (i + 1) * SP, :] = jnp.zeros((pad, D), BF)
            n1_s[i, S:SP, :] = jnp.where(
                lax.broadcasted_iota(jnp.int32, (pad, D), 0) == 0, 1.0, 0.0
            ).astype(BF)
        for cp in local:
            cp.wait()

        plan = {
            (1, 0): 1 * 6 + 0, (1, 1): 1 * 6 + 4, (1, 2): 2 * 6 + 4,
            (2, 0): 2 * 6 + 1, (2, 1): 2 * 6 + 5, (2, 2): 3 * 6 + 3,
            (3, 0): 2 * 6 + 5, (3, 1): 3 * 6 + 3, (3, 2): 3 * 6 + 5,
        }

        def tick(now):
            for (k, stage), when in plan.items():
                @pl.when(now == when)
                def _():
                    act(k, stage)

        def group(gidx, carry):
            def pair(p, carry):
                q = gidx * pairs + p
                tick(gidx * 6 + p)
                slot = q % 2
                for cp in fetch(q, slot):
                    cp.wait()

                @pl.when(q + 1 < nt * pairs)
                def _():
                    for cp in fetch(q + 1, (q + 1) % 2):
                        cp.start()

                grp = (t + 1 + gidx) % nt
                for e in range(2):
                    i = 2 * p + e
                    x = xb[slot, e].astype(F32)
                    scaled, _ = normal(x)
                    n1 = (scaled * g1_r[...] + b1_r[...]).astype(BF)
                    n1_s[i, 0:S, :] = n1
                    th = dot(w1t[...], n1) + tb1c[...]
                    ta = (th * cdf(th)).astype(BF)
                    ta_s[i] = ta
                    u = x + dot(w2t[...], ta) + tb2c[...]
                    u_s[i] = u
                    scaled, _ = normal(u)
                    at = pl.multiple_of(i * SP, 16)
                    n2[pl.ds(at, S), :] = (scaled * g2_r[...] + b2_r[...]).astype(BF)
                    valid = jnp.where(own * grp + i < cnt[0], 1.0, 0.0)
                    gp[pl.ds(at, S), :] = (gb[slot, e].astype(F32) * valid).astype(BF)
                return carry

            lax.fori_loop(0, pairs, pair, 0)

            def hidden(j, carry):
                tick(gidx * 6 + 3 + j)
                rr = pl.ds(pl.multiple_of(j * chunk, 16), chunk)
                ch = dot(n2[rr, :], W1[t]) + B1[t]
                da = dot_nt(gp[rr, :], W2[t])
                p = cdf(ch)
                ca[0, rr, :] = (ch * p).astype(BF)
                dh = (da * slope(ch, p)).astype(BF)
                dch[rr, :] = dh
                gcb1[...] += jnp.sum(dh.astype(F32), axis=0, keepdims=True)
                return carry

            lax.fori_loop(0, n_chunk, hidden, 0)
            gw2_r[...] += dot_tn(ca[0], gp[...])
            gw1_r[...] += dot_tn(n2[...], dch[...])
            return carry

        lax.fori_loop(0, nt, group, 0)

        def own_back(j, carry):
            rr = pl.ds(pl.multiple_of(j * chunk, 16), chunk)
            dacc[rr, :] = dot_nt(dch[rr, :], W1[t])
            return carry

        lax.fori_loop(0, n_chunk, own_back, 0)

        def other(k, carry):
            for kk in range(1, nt):
                @pl.when(k == kk)
                def _():
                    act(kk, 3)
            shard = (t + nt - k) % nt

            def hidden(j, carry):
                rr = pl.ds(pl.multiple_of(j * chunk, 16), chunk)
                ch = dot(n2[rr, :], W1[shard]) + B1[shard]
                da = dot_nt(gp[rr, :], W2[shard])
                p = cdf(ch)
                ca[k, rr, :] = (ch * p).astype(BF)
                dh = (da * slope(ch, p)).astype(BF)
                dacc[rr, :] += dot_nt(dh, W1[shard])
                return carry

            lax.fori_loop(0, n_chunk, hidden, 0)
            return carry

        lax.fori_loop(1, nt, other, 0)

        def xcopy(p, slot):
            return pltpu.make_async_copy(img.at[pl.ds(own * t + 2 * p, 2)], xb.at[slot], x_sem.at[slot])

        def gcopy(i, slot):
            return pltpu.make_async_copy(gi.at[slot], gim_h.at[i], i_sem.at[slot])

        xcopy(0, 0).start()

        def token(p, carry):
            slot = p % 2
            xcopy(p, slot).wait()

            @pl.when(p + 1 < pairs)
            def _():
                xcopy(p + 1, (p + 1) % 2).start()

            for e in range(2):
                i = 2 * p + e
                at = pl.multiple_of(i * SP, 16)
                dn2 = dacc[pl.ds(at, S), :]
                g = gp[pl.ds(at, S), :].astype(F32)
                scaled, inverse = normal(u_s[i])
                vec[0:1, :] += jnp.sum(dn2 * scaled, axis=0, keepdims=True)
                vec[1:2, :] += jnp.sum(dn2, axis=0, keepdims=True)
                vec[4:5, :] += jnp.sum(g, axis=0, keepdims=True)
                du = g + norm_back(dn2, g2_r[...], scaled, inverse)
                dz = du.astype(BF)
                tb2acc[...] += jnp.sum(dz.astype(F32), axis=1, keepdims=True)
                ta = ta_s[i]
                n1 = n1_s[i]
                sm_r[SP : SP + S, :] += dot_nt(dz, ta)
                th = dot(w1t[...], n1[0:S, :]) + tb1c[...]
                dth = (dot(tw2_r[...], dz) * slope(th, cdf(th))).astype(BF)
                sm_r[0:SP, :] += dot_nt(n1, dth)
                dn1 = dot(tw1_r[...], dth)
                scaled, inverse = normal(xb[slot, e].astype(F32))
                vec[2:3, :] += jnp.sum(dn1 * scaled, axis=0, keepdims=True)
                vec[3:4, :] += jnp.sum(dn1, axis=0, keepdims=True)

                @pl.when(p > 0)
                def _():
                    gcopy(i, e).wait()

                gi[e] = du + norm_back(dn1, g1_r[...], scaled, inverse)
                gcopy(i, e).start()
            return carry

        lax.fori_loop(0, pairs, token, 0)
        for e in range(2):
            gcopy(e, e).wait()

        low = 2 * SP
        for k in range(5):
            for h in range(2):
                sm_r[low + 2 * k + h : low + 2 * k + h + 1, :] = vec[k : k + 1, h * HD : (h + 1) * HD]
        sm_r[low + 10 : low + 11, 0:S] = jnp.sum(eye(S, F32) * tb2acc[...], axis=0, keepdims=True)
        for s in range(nt):
            for h in range(2):
                r = low + 11 + 2 * s + h
                sm_r[r : r + 1, :] = jnp.where(t == s, 1.0, 0.0) * gcb1[:, h * HD : (h + 1) * HD]

        def ocopy(j, slot):
            return pltpu.make_async_copy(ob.at[slot], out_h.at[pl.ds(2 * j, 2)], o_sem.at[slot])

        def result(j, carry):
            slot = j % 2
            rr = pl.ds(pl.multiple_of(j * chunk, 16), chunk)
            total = dot(ca[0, rr, :], W2[t])
            for k in range(1, nt):
                total += dot(ca[k, rr, :], W2[(t + nt - k) % nt])

            @pl.when(j >= 2)
            def _():
                ocopy(j, slot).wait()

            for e in range(2):
                v = total[e * SP : e * SP + S, :] + u_s[2 * j + e] + cb2_r[...]
                ob[slot, e] = v.astype(BF)
            ocopy(j, slot).start()
            return carry

        lax.fori_loop(0, n_chunk, result, 0)
        for slot in range(2):
            ocopy(slot, slot).wait()

    V = pltpu.VMEM
    DMA = pltpu.SemaphoreType.DMA
    any_ = pl.BlockSpec(memory_space=pl.ANY)
    vm = pl.BlockSpec(memory_space=V)
    out = pl.pallas_call(
        kernel,
        out_shape=(
            jax.ShapeDtypeStruct((own, S, D), BF),
            jax.ShapeDtypeStruct((own, S, D), F32),
            jax.ShapeDtypeStruct((D, H), F32),
            jax.ShapeDtypeStruct((H, D), F32),
            jax.ShapeDtypeStruct((SM, DS), F32),
        ),
        in_specs=[any_, any_, any_, any_, vm, pl.BlockSpec(memory_space=pltpu.SMEM)] + [vm] * 9,
        out_specs=(any_, any_, vm, vm, vm),
        scratch_shapes=[
            V((nt, D, H), BF), V((nt, H, D), BF), V((nt, 1, H), F32),
            V((2, 2, S, D), BF), V((2, 2, S, D), BF),
            V((rows, D), BF), V((rows, D), BF), V((nt, rows, H), BF), V((rows, H), BF), V((rows, D), F32),
            V((own, S, D), F32), V((own, DS, D), BF), V((own, SP, D), BF),
            V((DS, S), BF), V((S, DS), BF), V((DS, 1), F32), V((S, 1), F32),
            V((1, H), F32), V((8, D), F32), V((S, 1), F32),
            V((2, 2, S, D), BF), V((2, S, D), F32),
            DMA((2,)), DMA((2,)), DMA((2,)), DMA((2,)), DMA((2,)),
            DMA((nt, 2)), DMA((nt, 2)), DMA((nt, 7, 2)), DMA((nt, 7, 2)), DMA((nt,)), DMA((nt,)),
        ],
        compiler_params=pltpu.CompilerParams(
            collective_id=0, has_side_effects=True, vmem_limit_bytes=61 * 2**20
        ),
    )(
        images, cot, cw1, cw2, cb1.reshape(1, H), counts,
        g1.reshape(1, D), b1.reshape(1, D), g2.reshape(1, D), b2.reshape(1, D),
        tw1, tw2, tb1.reshape(1, DS), tb2.reshape(1, S), cb2.reshape(1, D),
    )
    output, grad_images, gw1, gw2, small = out
    gw1, gw2 = lax.psum((gw1, gw2), "batch")
    small = lax.psum(small, ("batch", "tensor"))
    low = 2 * SP
    vecs = small[low : low + 10].reshape(5, D)
    r = low + 11 + 2 * lax.axis_index("tensor")
    gcb1 = lax.dynamic_slice_in_dim(small, r, 2, 0).reshape(H)
    return (
        output, grad_images,
        vecs[2], vecs[3],
        small[0:S], small[S], small[SP : SP + S].T, small[low + 10, :S],
        vecs[0], vecs[1],
        gw1, gcb1, gw2, vecs[4],
    )


def solution(mesh):
    nb, nt = mesh.shape["batch"], mesh.shape["tensor"]
    in_specs = (
        P("batch", None, None), P("batch"),
        P(), P(), P(), P(), P(), P(), P(), P(),
        P(None, "tensor"), P("tensor"), P("tensor", None), P(),
        P("batch", None, None),
    )
    both = P(("batch", "tensor"), None, None)
    out_specs = (
        both, both,
        P(), P(), P(), P(), P(), P(), P(), P(),
        P(None, "tensor"), P("tensor"), P("tensor", None), P(),
    )
    return jax.shard_map(
        lambda *args: per_device(nb, nt, args),
        mesh=mesh, in_specs=in_specs, out_specs=out_specs, check_vma=False,
    )
```

```python
import jax
import jax.numpy as jnp
from jax import lax
from jax.experimental import pallas as pl
from jax.experimental.pallas import tpu as pltpu
from jax.sharding import PartitionSpec as P

EPSILON = 1e-06
ROOT_HALF = 0.7071067811865476
INV_ROOT_TAU = 0.3989422804014327
MESH = pl.DeviceIdType.MESH
BF = jnp.bfloat16
F32 = jnp.float32
RING = 8


def dot(a, b):
    return lax.dot_general(a, b, (((1,), (0,)), ((), ())), preferred_element_type=F32)


def dot_nt(a, b):
    return lax.dot_general(a, b, (((1,), (1,)), ((), ())), preferred_element_type=F32)


def dot_tn(a, b):
    return lax.dot_general(a, b, (((0,), (0,)), ((), ())), preferred_element_type=F32)


def flip(v, bit):
    step = 1 << bit
    return v + (1 - 2 * ((v // step) % 2)) * step


def normal(v):
    center = v - jnp.mean(v, axis=-1, keepdims=True)
    inverse = lax.rsqrt(jnp.mean(center * center, axis=-1, keepdims=True) + EPSILON)
    return center * inverse, inverse


def cdf(v):
    return 0.5 * (1.0 + lax.erf(v * ROOT_HALF))


def slope(v, p):
    return p + v * jnp.exp(-0.5 * v * v) * INV_ROOT_TAU


def norm_back(grad, gain, scaled, inverse):
    weighted = grad * gain
    return inverse * (
        weighted
        - jnp.mean(weighted, axis=-1, keepdims=True)
        - scaled * jnp.mean(weighted * scaled, axis=-1, keepdims=True)
    )


def eye(n, dtype):
    rows = lax.broadcasted_iota(jnp.int32, (n, n), 0)
    cols = lax.broadcasted_iota(jnp.int32, (n, n), 1)
    return jnp.where(rows == cols, 1.0, 0.0).astype(dtype)


def column(row):
    n = row.shape[1]
    return jnp.sum(eye(n, F32) * row, axis=1, keepdims=True)


def per_device(nb, nt, args):
    (images, counts, g1, b1, tw1, tb1, tw2, tb2, g2, b2, cw1, cb1, cw2, cb2, cot) = args
    slots, S, D = images.shape
    DS = tw1.shape[1]
    H = cw1.shape[1]
    own = slots // nt
    SP = -(-S // 16) * 16
    pairs = own // 2
    rows = own * SP
    chunk = 2 * SP
    n_chunk = rows // chunk
    piece = D // RING
    SM = 512
    HD = D // 2

    def kernel(
        img, cot_h, w1_h, w2_h, cb1_1, cnt, g1_1, b1_1, g2_1, b2_1, tw1_r, w2t, tb1_1, tb2_1, cb2_1,
        out_h, gim_h, gw1_o, gw2_o, gg1_o, gb1_o, gtw1_o, gtb1_o, gtw2_o, gtb2_o, gg2_o, gb2_o, gcb1_o, gcb2_o,
        W1, W2, B1, xb, gb, n2, gp, ca, dch, dacc, u_s, ta_s, n1_s, w1t, tw2_r, tb1c, tb2c, gcb1, vec, tb2acc, ob, gi,
        cb1_r, g1_r, b1_r, g2_r, b2_r, cb2_r, acc, sm_r, snd0, rcv0, snd1, rcv1, snd2, rcv2, sndx, rcvx, gwb,
        s_snd, s_rcv, s_mid, z_snd, z_rcv, x_snd, x_rcv, s_all,
        x_sem, g_sem, l_sem, o_sem, i_sem, zs, zr, ps, pr, bs, br,
        as_, ar_, axs, axr, sps, spr, szs, szr, sxs, sxr, sys_, syr, sqs, sqr,
    ):
        b = lax.axis_index("batch")
        t = lax.axis_index("tensor")
        l = b % RING
        base = b - l
        c = l % 2
        lf, ls = flip(l, 1), flip(l, 2)
        p_first = (1 - c) * lf + c * ls
        p_second = (1 - c) * ls + c * lf
        p_both = flip(flip(l, 1), 2)
        p_core = flip(l, 0)
        zpeer = [(t + k) % nt for k in range(1, nt)]
        extra = range(3, nb.bit_length() - 1)

        bar = pltpu.get_barrier_semaphore()
        partners = [(b, z) for z in zpeer]
        partners += [(base + (l + k) % RING, t) for k in range(1, RING)]
        partners += [(flip(b, e), t) for e in extra]
        for d in partners:
            pl.semaphore_signal(bar, inc=1, device_id=d, device_id_type=MESH)

        def fetch(q, slot):
            grp = (t + 1 + q // pairs) % nt
            start = own * grp + 2 * (q % pairs)
            return (
                pltpu.make_async_copy(img.at[pl.ds(start, 2)], xb.at[slot], x_sem.at[slot]),
                pltpu.make_async_copy(cot_h.at[pl.ds(start, 2)], gb.at[slot], g_sem.at[slot]),
            )

        for cp in fetch(0, 0):
            cp.start()
        local = [
            pltpu.make_async_copy(w1_h, W1.at[t], l_sem.at[0]),
            pltpu.make_async_copy(w2_h, W2.at[t], l_sem.at[1]),
        ]
        for cp in local:
            cp.start()
        cb1_r[...] = cb1_1[...].reshape(1, H)
        for ref, one in ((g1_r, g1_1), (b1_r, b1_1), (g2_r, g2_1), (b2_r, b2_1), (cb2_r, cb2_1)):
            ref[...] = one[...].reshape(1, D)
        B1[t] = cb1_r[...]

        pl.semaphore_wait(bar, len(partners))

        mine = pl.ds(pl.multiple_of(l * piece, piece), piece)

        def z_copy(k, arr):
            src = (w1_h, w2_h)[arr].at[mine]
            dst = (W1, W2)[arr].at[t, mine]
            return pltpu.make_async_remote_copy(
                src, dst, zs.at[k, arr], zr.at[k, arr], device_id=(b, (t + k) % nt), device_id_type=MESH
            )

        def b_copy(k):
            return pltpu.make_async_remote_copy(
                cb1_r, B1.at[t], bs.at[k], br.at[k], device_id=(b, (t + k) % nt), device_id_type=MESH
            )

        for k in range(1, nt):
            for arr in range(2):
                z_copy(k, arr).start()
            b_copy(k).start()

        def plane(k, stage):
            shard = (t + nt - k) % nt
            first = (l,) if stage == 0 else (l, p_first) if stage == 1 else (l, p_first, p_second, p_both)
            peer = (p_first, p_second, p_core)[stage]
            at = (0, 1, 3)[stage]
            copies = []
            for j, who in enumerate(first):
                part = pl.ds(pl.multiple_of(who * piece, piece), piece)
                for arr in range(2):
                    ref = (W1, W2)[arr].at[shard, part]
                    copies.append(
                        pltpu.make_async_remote_copy(
                            ref, ref, ps.at[k, at + j, arr], pr.at[k, at + j, arr],
                            device_id=(base + peer, t), device_id_type=MESH,
                        )
                    )
            return copies

        def act(k, stage):
            if stage == 0:
                for arr in range(2):
                    z_copy(k, arr).wait()
                b_copy(k).wait()
            else:
                for cp in plane(k, stage - 1):
                    cp.wait()
            if stage < 3:
                for cp in plane(k, stage):
                    cp.start()

        w1t[...] = dot_nt(eye(DS, BF), tw1_r[...]).astype(BF)
        tw2_r[...] = dot_nt(eye(DS, BF), w2t[...]).astype(BF)
        tb1c[...] = column(tb1_1[...].reshape(1, DS))
        tb2c[...] = column(tb2_1[...].reshape(1, S))
        acc[...] = jnp.zeros_like(acc)
        gcb1[...] = jnp.zeros_like(gcb1)
        vec[...] = jnp.zeros_like(vec)
        tb2acc[...] = jnp.zeros_like(tb2acc)
        sm_r[...] = jnp.zeros_like(sm_r)
        pad = SP - S
        for i in range(own):
            n2[i * SP + S : (i + 1) * SP, :] = jnp.zeros((pad, D), BF)
            gp[i * SP + S : (i + 1) * SP, :] = jnp.zeros((pad, D), BF)
            n1_s[i, S:SP, :] = jnp.where(
                lax.broadcasted_iota(jnp.int32, (pad, D), 0) == 0, 1.0, 0.0
            ).astype(BF)
        for cp in local:
            cp.wait()

        plan = {
            (1, 0): 1 * 6 + 0, (1, 1): 1 * 6 + 4, (1, 2): 2 * 6 + 4,
            (2, 0): 2 * 6 + 1, (2, 1): 2 * 6 + 5, (2, 2): 3 * 6 + 3,
            (3, 0): 2 * 6 + 5, (3, 1): 3 * 6 + 3, (3, 2): 3 * 6 + 5,
        }

        def tick(now):
            for (k, stage), when in plan.items():
                @pl.when(now == when)
                def _():
                    act(k, stage)

        def group(gidx, carry):
            def pair(p, carry):
                q = gidx * pairs + p
                tick(gidx * 6 + p)
                slot = q % 2
                for cp in fetch(q, slot):
                    cp.wait()

                @pl.when(q + 1 < nt * pairs)
                def _():
                    for cp in fetch(q + 1, (q + 1) % 2):
                        cp.start()

                grp = (t + 1 + gidx) % nt
                for e in range(2):
                    i = 2 * p + e
                    x = xb[slot, e].astype(F32)
                    scaled, _ = normal(x)
                    n1 = (scaled * g1_r[...] + b1_r[...]).astype(BF)
                    n1_s[i, 0:S, :] = n1
                    th = dot(w1t[...], n1) + tb1c[...]
                    ta = (th * cdf(th)).astype(BF)
                    ta_s[i] = ta
                    u = x + dot(w2t[...], ta) + tb2c[...]
                    u_s[i] = u
                    scaled, _ = normal(u)
                    at = pl.multiple_of(i * SP, 16)
                    n2[pl.ds(at, S), :] = (scaled * g2_r[...] + b2_r[...]).astype(BF)
                    valid = jnp.where(own * grp + i < cnt[0], 1.0, 0.0)
                    gp[pl.ds(at, S), :] = (gb[slot, e].astype(F32) * valid).astype(BF)
                return carry

            lax.fori_loop(0, pairs, pair, 0)

            def hidden(j, carry):
                tick(gidx * 6 + 3 + j)
                rr = pl.ds(pl.multiple_of(j * chunk, 16), chunk)
                ch = dot(n2[rr, :], W1[t]) + B1[t]
                da = dot_nt(gp[rr, :], W2[t])
                p = cdf(ch)
                ca[0, rr, :] = (ch * p).astype(BF)
                dh = (da * slope(ch, p)).astype(BF)
                dch[rr, :] = dh
                gcb1[...] += jnp.sum(dh.astype(F32), axis=0, keepdims=True)
                return carry

            lax.fori_loop(0, n_chunk, hidden, 0)
            acc[1] += dot_tn(ca[0], gp[...])
            acc[0] += dot_tn(n2[...], dch[...])
            return carry

        lax.fori_loop(0, nt, group, 0)

        half, quarter, eighth = D, D // 2, D // 4
        bit_f = (1 - c) * ((l // 2) % 2) + c * ((l // 4) % 2)
        bit_s = (1 - c) * ((l // 4) % 2) + c * ((l // 2) % 2)
        row_f = pl.multiple_of(bit_f * quarter, eighth)
        row_fo = pl.multiple_of((1 - bit_f) * quarter, eighth)
        row_s = pl.multiple_of(bit_f * quarter + bit_s * eighth, eighth)
        row_so = pl.multiple_of(bit_f * quarter + (1 - bit_s) * eighth, eighth)

        def remote(src, dst, ss, rs, dev):
            return pltpu.make_async_remote_copy(src, dst, ss, rs, device_id=dev, device_id_type=MESH)

        def sum_copy(stage):
            if stage < 3:
                src, dst = ((snd0, rcv0), (snd1, rcv1), (snd2, rcv2))[stage]
                peer = (p_core, p_first, p_second)[stage]
            else:
                src = (
                    gwb.at[c, pl.ds(row_s, eighth)], gwb.at[c, pl.ds(row_f, quarter)], gwb.at[c],
                )[stage - 3]
                dst = src
                peer = (p_second, p_first, p_core)[stage - 3]
            return remote(src, dst, as_.at[stage], ar_.at[stage], (base + peer, t))

        def sum_step(stage):
            if stage > 0:
                sum_copy(stage - 1).wait()
            if stage == 0:
                snd0[...] = acc[1 - c].astype(BF)
            elif stage == 1:
                mine = pl.ds(row_f, quarter)
                theirs = pl.ds(row_fo, quarter)
                snd1[...] = (acc[c, theirs, :] + rcv0[theirs, :].astype(F32)).astype(BF)
                sum_copy(1).start()
                acc[c, mine, :] += rcv0[mine, :].astype(F32)
            elif stage == 2:
                other_q = pl.multiple_of((1 - bit_s) * eighth, eighth)
                snd2[...] = (acc[c, pl.ds(row_so, eighth), :] + rcv1[pl.ds(other_q, eighth), :].astype(F32)).astype(BF)
                sum_copy(2).start()
                this_q = pl.multiple_of(bit_s * eighth, eighth)
                acc[c, pl.ds(row_s, eighth), :] += rcv1[pl.ds(this_q, eighth), :].astype(F32)
            elif stage == 3:
                total = acc[c, pl.ds(row_s, eighth), :] + rcv2[...].astype(F32)
                for n, e in enumerate(extra):
                    sndx[n] = total.astype(BF)
                    cp = remote(sndx.at[n], rcvx.at[n], axs.at[n], axr.at[n], (flip(b, e), t))
                    cp.start()
                    cp.wait()
                    total = sndx[n].astype(F32) + rcvx[n].astype(F32)
                gwb[c, pl.ds(row_s, eighth), :] = total.astype(BF)
            if stage in (0, 3, 4, 5):
                sum_copy(stage).start()

        late = {1: 1, 2: 5, 3: 8, 4: 11, 5: 14}

        def late_tick(now):
            for stage, when in late.items():
                @pl.when(now == when)
                def _():
                    sum_step(stage)

        sum_step(0)

        def own_back(j, carry):
            rr = pl.ds(pl.multiple_of(j * chunk, 16), chunk)
            dacc[rr, :] = dot_nt(dch[rr, :], W1[t])
            return carry

        lax.fori_loop(0, n_chunk, own_back, 0)

        def other(k, carry):
            for kk in range(1, nt):
                @pl.when(k == kk)
                def _():
                    act(kk, 3)
            shard = (t + nt - k) % nt

            def hidden(j, carry):
                late_tick((k - 1) * n_chunk + j)
                rr = pl.ds(pl.multiple_of(j * chunk, 16), chunk)
                ch = dot(n2[rr, :], W1[shard]) + B1[shard]
                da = dot_nt(gp[rr, :], W2[shard])
                p = cdf(ch)
                ca[k, rr, :] = (ch * p).astype(BF)
                dh = (da * slope(ch, p)).astype(BF)
                dacc[rr, :] += dot_nt(dh, W1[shard])
                return carry

            lax.fori_loop(0, n_chunk, hidden, 0)
            return carry

        lax.fori_loop(1, nt, other, 0)

        def xcopy(p, slot):
            return pltpu.make_async_copy(img.at[pl.ds(own * t + 2 * p, 2)], xb.at[slot], x_sem.at[slot])

        def gcopy(i, slot):
            return pltpu.make_async_copy(gi.at[slot], gim_h.at[i], i_sem.at[slot])

        xcopy(0, 0).start()

        def token(p, carry):
            slot = p % 2
            late_tick((nt - 1) * n_chunk + p)
            xcopy(p, slot).wait()

            @pl.when(p + 1 < pairs)
            def _():
                xcopy(p + 1, (p + 1) % 2).start()

            for e in range(2):
                i = 2 * p + e
                at = pl.multiple_of(i * SP, 16)
                dn2 = dacc[pl.ds(at, S), :]
                g = gp[pl.ds(at, S), :].astype(F32)
                scaled, inverse = normal(u_s[i])
                vec[0:1, :] += jnp.sum(dn2 * scaled, axis=0, keepdims=True)
                vec[1:2, :] += jnp.sum(dn2, axis=0, keepdims=True)
                vec[4:5, :] += jnp.sum(g, axis=0, keepdims=True)
                du = g + norm_back(dn2, g2_r[...], scaled, inverse)
                dz = du.astype(BF)
                tb2acc[...] += jnp.sum(dz.astype(F32), axis=1, keepdims=True)
                ta = ta_s[i]
                n1 = n1_s[i]
                sm_r[SP : SP + S, :] += dot_nt(dz, ta)
                th = dot(w1t[...], n1[0:S, :]) + tb1c[...]
                dth = (dot(tw2_r[...], dz) * slope(th, cdf(th))).astype(BF)
                sm_r[0:SP, :] += dot_nt(n1, dth)
                dn1 = dot(tw1_r[...], dth)
                scaled, inverse = normal(xb[slot, e].astype(F32))
                vec[2:3, :] += jnp.sum(dn1 * scaled, axis=0, keepdims=True)
                vec[3:4, :] += jnp.sum(dn1, axis=0, keepdims=True)

                @pl.when(p > 0)
                def _():
                    gcopy(i, e).wait()

                gi[e] = du + norm_back(dn1, g1_r[...], scaled, inverse)
                gcopy(i, e).start()
            return carry

        lax.fori_loop(0, pairs, token, 0)
        for e in range(2):
            gcopy(e, e).wait()

        low = 2 * SP
        for k in range(5):
            for h in range(2):
                sm_r[low + 2 * k + h : low + 2 * k + h + 1, :] = vec[k : k + 1, h * HD : (h + 1) * HD]
        sm_r[low + 10 : low + 11, 0:S] = jnp.sum(eye(S, F32) * tb2acc[...], axis=0, keepdims=True)
        for s in range(nt):
            for h in range(2):
                r = low + 11 + 2 * s + h
                sm_r[r : r + 1, :] = jnp.where(t == s, 1.0, 0.0) * gcb1[:, h * HD : (h + 1) * HD]

        part, small = SM // RING, SM // RING // nt
        s_snd[...] = sm_r[...].astype(BF)

        def eighths(k, back):
            whom = (base + (l + k) % RING, t)
            if back:
                ref = s_all.at[pl.ds(pl.multiple_of(l * part, part), part)]
                return remote(ref, ref, sqs.at[k], sqr.at[k], whom)
            src = s_snd.at[pl.ds(pl.multiple_of(((l + k) % RING) * part, part), part)]
            return remote(src, s_rcv.at[k], sps.at[k], spr.at[k], whom)

        def quarters(k, back):
            whom = (b, (t + k) % nt)
            if back:
                ref = s_all.at[pl.ds(pl.multiple_of(l * part + t * small, small), small)]
                return remote(ref, ref, sys_.at[k], syr.at[k], whom)
            src = z_snd.at[pl.ds(pl.multiple_of(((t + k) % nt) * small, small), small)]
            return remote(src, z_rcv.at[k], szs.at[k], szr.at[k], whom)

        for k in range(1, RING):
            eighths(k, False).start()

        def small_step(stage):
            if stage == 1:
                total = sm_r[pl.ds(pl.multiple_of(l * part, part), part), :]
                for k in range(1, RING):
                    eighths(k, False).wait()
                    total += s_rcv[k].astype(F32)
                s_mid[...] = total
                z_snd[...] = total.astype(BF)
                for k in range(1, nt):
                    quarters(k, False).start()
            elif stage == 2:
                total = s_mid[pl.ds(pl.multiple_of(t * small, small), small), :]
                for k in range(1, nt):
                    quarters(k, False).wait()
                    total += z_rcv[k].astype(F32)
                for n, e in enumerate(extra):
                    x_snd[n] = total.astype(BF)
                    cp = remote(x_snd.at[n], x_rcv.at[n], sxs.at[n], sxr.at[n], (flip(b, e), t))
                    cp.start()
                    cp.wait()
                    total = x_snd[n].astype(F32) + x_rcv[n].astype(F32)
                s_all[pl.ds(pl.multiple_of(l * part + t * small, small), small), :] = total.astype(BF)
                for k in range(1, nt):
                    quarters(k, True).start()
            elif stage == 3:
                for k in range(1, nt):
                    quarters(k, True).wait()
                for k in range(1, RING):
                    eighths(k, True).start()
            else:
                for k in range(1, RING):
                    eighths(k, True).wait()

        def ocopy(j, slot):
            return pltpu.make_async_copy(ob.at[slot], out_h.at[pl.ds(2 * j, 2)], o_sem.at[slot])

        def result(j, carry):
            slot = j % 2
            late_tick((nt - 1) * n_chunk + pairs + j)

            @pl.when(j == 2)
            def _():
                small_step(1)

            rr = pl.ds(pl.multiple_of(j * chunk, 16), chunk)
            total = dot(ca[0, rr, :], W2[t])
            for k in range(1, nt):
                total += dot(ca[k, rr, :], W2[(t + nt - k) % nt])

            @pl.when(j >= 2)
            def _():
                ocopy(j, slot).wait()

            for e in range(2):
                v = total[e * SP : e * SP + S, :] + u_s[2 * j + e] + cb2_r[...]
                ob[slot, e] = v.astype(BF)
            ocopy(j, slot).start()
            return carry

        lax.fori_loop(0, n_chunk, result, 0)
        small_step(2)
        for slot in range(2):
            ocopy(slot, slot).wait()
        sum_copy(5).wait()
        acc[...] = gwb[...].astype(F32)
        flush = [
            pltpu.make_async_copy(acc.at[0], gw1_o, l_sem.at[0]),
            pltpu.make_async_copy(acc.at[1], gw2_o, l_sem.at[1]),
        ]
        for cp in flush:
            cp.start()
        small_step(3)
        small_step(4)
        gtw1_o[...] = s_all[0:S, :].astype(F32)
        gtw2_o[...] = s_all[SP : SP + S, :].astype(F32)
        ends = s_all[low : low + 32, :].astype(F32)
        gtb1_o[...] = s_all[S - 4 : S + 12, :].astype(F32)[4]
        gtb2_o[...] = ends[10, 0:S]
        for k, ref in enumerate((gg2_o, gb2_o, gg1_o, gb1_o, gcb2_o)):
            for h in range(2):
                ref[h * HD : (h + 1) * HD] = ends[2 * k + h]
        for h in range(2):
            total = ends[11 + h] * jnp.where(t == 0, 1.0, 0.0)
            for s in range(1, nt):
                total += ends[11 + 2 * s + h] * jnp.where(t == s, 1.0, 0.0)
            gcb1_o[h * HD : (h + 1) * HD] = total
        for cp in flush:
            cp.wait()

    V = pltpu.VMEM
    DMA = pltpu.SemaphoreType.DMA
    any_ = pl.BlockSpec(memory_space=pl.ANY)
    vm = pl.BlockSpec(memory_space=V)
    f = lambda *shape: jax.ShapeDtypeStruct(shape, F32)
    xb = max(1, nb.bit_length() - 4)
    part, small = SM // RING, SM // RING // nt
    out = pl.pallas_call(
        kernel,
        out_shape=(
            jax.ShapeDtypeStruct((own, S, D), BF), f(own, S, D), f(D, H), f(H, D),
            f(D), f(D), f(S, DS), f(DS), f(S, DS), f(S), f(D), f(D), f(H), f(D),
        ),
        in_specs=[any_, any_, any_, any_, vm, pl.BlockSpec(memory_space=pltpu.SMEM)] + [vm] * 9,
        out_specs=(any_,) * 4 + (vm,) * 10,
        scratch_shapes=[
            V((nt, D, H), BF), V((nt, H, D), BF), V((nt, 1, H), F32),
            V((2, 2, S, D), BF), V((2, 2, S, D), BF),
            V((rows, D), BF), V((rows, D), BF), V((nt, rows, H), BF), V((rows, H), BF), V((rows, D), F32),
            V((own, S, D), F32), V((own, DS, D), BF), V((own, SP, D), BF),
            V((DS, S), BF), V((DS, S), BF), V((DS, 1), F32), V((S, 1), F32),
            V((1, H), F32), V((8, D), F32), V((S, 1), F32),
            V((2, 2, S, D), BF), V((2, S, D), F32),
            V((1, H), F32), V((1, D), F32), V((1, D), F32), V((1, D), F32), V((1, D), F32), V((1, D), F32),
            V((2, D, D), F32), V((SM, DS), F32),
            V((D, D), BF), V((D, D), BF), V((D // 2, D), BF), V((D // 2, D), BF), V((D // 4, D), BF), V((D // 4, D), BF),
            V((xb, D // 4, D), BF), V((xb, D // 4, D), BF), V((2, D, D), BF),
            V((SM, DS), BF), V((RING, part, DS), BF), V((part, DS), F32), V((part, DS), BF), V((nt, small, DS), BF),
            V((xb, small, DS), BF), V((xb, small, DS), BF), V((SM, DS), BF),
            DMA((2,)), DMA((2,)), DMA((2,)), DMA((2,)), DMA((2,)),
            DMA((nt, 2)), DMA((nt, 2)), DMA((nt, 7, 2)), DMA((nt, 7, 2)), DMA((nt,)), DMA((nt,)),
            DMA((6,)), DMA((6,)), DMA((xb,)), DMA((xb,)), DMA((RING,)), DMA((RING,)), DMA((nt,)), DMA((nt,)),
            DMA((xb,)), DMA((xb,)), DMA((nt,)), DMA((nt,)), DMA((RING,)), DMA((RING,)),
        ],
        compiler_params=pltpu.CompilerParams(
            collective_id=0, has_side_effects=True, vmem_limit_bytes=61 * 2**20
        ),
    )(images, cot, cw1, cw2, cb1, counts, g1, b1, g2, b2, tw1, tw2.T, tb1, tb2, cb2)
    out = list(out)
    out[6 + 2] = out[8].T
    return (
        out[0], out[1], out[4], out[5], out[6], out[7], out[8], out[9],
        out[10], out[11], out[2], out[12], out[3], out[13],
    )


def solution(mesh):
    nb, nt = mesh.shape["batch"], mesh.shape["tensor"]
    in_specs = (
        P("batch", None, None), P("batch"),
        P(), P(), P(), P(), P(), P(), P(), P(),
        P(None, "tensor"), P("tensor"), P("tensor", None), P(),
        P("batch", None, None),
    )
    both = P(("batch", "tensor"), None, None)
    out_specs = (
        both, both,
        P(), P(), P(), P(), P(), P(), P(), P(),
        P(None, "tensor"), P("tensor"), P("tensor", None), P(),
    )
    return jax.shard_map(
        lambda *args: per_device(nb, nt, args),
        mesh=mesh, in_specs=in_specs, out_specs=out_specs, check_vma=False,
    )
```

```python
import jax
import jax.numpy as jnp
from jax import lax
from jax.experimental import pallas as pl
from jax.experimental.pallas import tpu as pltpu
from jax.sharding import PartitionSpec as P

EPSILON = 1e-06
ROOT_HALF = 0.7071067811865476
INV_ROOT_TAU = 0.3989422804014327
LOG2_E = 1.4426950408889634
MESH = pl.DeviceIdType.MESH
BF = jnp.bfloat16
F32 = jnp.float32
SLOTS = 4
RING = 8
SMALL = 512


def dot(a, b):
    return lax.dot_general(a, b, (((1,), (0,)), ((), ())), preferred_element_type=F32)


def dot_nt(a, b):
    return lax.dot_general(a, b, (((1,), (1,)), ((), ())), preferred_element_type=F32)


def dot_tn(a, b):
    return lax.dot_general(a, b, (((0,), (0,)), ((), ())), preferred_element_type=F32)


def flip(v, bit):
    step = 1 << bit
    return v + (1 - 2 * ((v // step) % 2)) * step


def normal(v):
    center = v - jnp.mean(v, axis=-1, keepdims=True)
    inverse = lax.rsqrt(jnp.mean(center * center, axis=-1, keepdims=True) + EPSILON)
    return center * inverse, inverse


def gelu_parts(v):
    s = v * ROOT_HALF
    return 1.0 + lax.erf(s), s


def slope_twice(r, s):
    return r + (s * jnp.exp2(s * s * -LOG2_E)) * (2.0 * INV_ROOT_TAU / ROOT_HALF)


def norm_back(grad, gain, scaled, inverse):
    weighted = grad * gain
    return inverse * (
        weighted
        - jnp.mean(weighted, axis=-1, keepdims=True)
        - scaled * jnp.mean(weighted * scaled, axis=-1, keepdims=True)
    )


def eye(n, dtype, value=1.0):
    rows = lax.broadcasted_iota(jnp.int32, (n, n), 0)
    cols = lax.broadcasted_iota(jnp.int32, (n, n), 1)
    return jnp.where(rows == cols, value, 0.0).astype(dtype)


def column(row):
    n = row.shape[1]
    return jnp.sum(eye(n, F32) * row, axis=1, keepdims=True)


def total_of(v):
    return jnp.sum(v, axis=0, keepdims=True)


def per_device(nb, nt, args):
    (images, counts, g1, b1, tw1, tb1, tw2, tb2, g2, b2, cw1, cb1, cw2, cb2, cot) = args
    slots, S, D = images.shape
    DS = tw1.shape[1]
    H = cw1.shape[1]
    own = slots // nt
    SP = -(-S // 16) * 16
    pairs = own // 2
    rows = own * SP
    chunk = 2 * SP
    n_chunk = rows // chunk
    third = D // pairs
    piece = D // RING
    HD = D // 2
    near = [sorted((s for s in range(nt) if s != t), key=lambda s: (abs(s - t), s)) for t in range(nt)]
    if nt == 4:
        near[2] = [3, 1, 0]
    extra = range(3, nb.bit_length() - 1)

    def kernel(
        img, cot_h, w1_h, w2_h, cb1_1, cnt, g1_1, b1_1, g2_1, b2_1, tw1_r, w2t_r, tb1_1, tb2_1, cb2_1,
        out_h, gim_h, gwb_o, s_all,
        W1, W2, B1, xb, gb, n2a, n2b, gpa, gpb, ca, dch, dacc, u_s, ta_s, n1_s, w1t, w2t, tw2_r, tb1c, tb2c,
        gcb1, vec, tb2acc, outs,
        cb1_r, g1_r, b1_r, g2_r, b2_r, cb2_r, acc, sm_r, rcv0, rcv1, rcv2, sndx, rcvx, gwb,
        s_snd, s_rcv, s_mid, z_snd, z_rcv, x_snd, x_rcv,
        x_sem, g_sem, l_sem, o_sem, i_sem, zs, zr, ps, pr, bs, br,
        as_, ar_, axs, axr, sps, spr, szs, szr, sxs, sxr, sys_, syr, sqs, sqr,
    ):
        b = lax.axis_index("batch")
        t = lax.axis_index("tensor")
        l = b % RING
        base = b - l
        c = l % 2
        lf, ls = flip(l, 1), flip(l, 2)
        p_first = (1 - c) * lf + c * ls
        p_second = (1 - c) * ls + c * lf
        p_both = flip(flip(l, 1), 2)
        p_core = flip(l, 0)

        def remote(src, dst, ss, rs, dev):
            return pltpu.make_async_remote_copy(src, dst, ss, rs, device_id=dev, device_id_type=MESH)

        bar = pltpu.get_barrier_semaphore()
        partners = [(b, (t + k) % nt) for k in range(1, nt)]
        partners += [(base + (l + k) % RING, t) for k in range(1, RING)]
        partners += [(flip(b, e), t) for e in extra]
        for d in partners:
            pl.semaphore_signal(bar, inc=1, device_id=d, device_id_type=MESH)

        def fetch(q, slot):
            grp = (t + 1 + q // pairs) % nt
            at = pl.ds(own * grp + 2 * (q % pairs), 2)
            return (
                pltpu.make_async_copy(img.at[at], xb.at[slot], x_sem.at[slot]),
                pltpu.make_async_copy(cot_h.at[at], gb.at[slot], g_sem.at[slot]),
            )

        for q in range(SLOTS - 1):
            for cp in fetch(q, q):
                cp.start()
        local = [
            pltpu.make_async_copy(w1_h, W1.at[t], l_sem.at[0]),
            pltpu.make_async_copy(w2_h, W2.at[t], l_sem.at[1]),
        ]
        for cp in local:
            cp.start()

        cb1_r[...] = cb1_1[...].reshape(1, H)
        for ref, one in ((g1_r, g1_1), (b1_r, b1_1), (g2_r, g2_1), (b2_r, b2_1), (cb2_r, cb2_1)):
            ref[...] = one[...].reshape(1, D)
        B1[t] = cb1_r[...]
        w1t[...] = dot_nt(eye(DS, BF), tw1_r[...]).astype(BF)
        w2t[...] = (w2t_r[...].astype(F32) * 0.5).astype(BF)
        tw2_r[...] = dot_nt(eye(DS, BF), w2t[...]).astype(BF)
        tb1c[...] = column(tb1_1[...].reshape(1, DS))
        tb2c[...] = column(tb2_1[...].reshape(1, S))
        acc[...] = jnp.zeros_like(acc)
        gcb1[...] = jnp.zeros_like(gcb1)
        vec[...] = jnp.zeros_like(vec)
        tb2acc[...] = jnp.zeros_like(tb2acc)
        sm_r[...] = jnp.zeros_like(sm_r)
        pad = SP - S
        for i in range(own):
            for ref in (n2a, n2b, gpa, gpb):
                ref[i * SP + S : (i + 1) * SP, :] = jnp.zeros((pad, D), BF)
            n1_s[i, S:SP, :] = jnp.where(
                lax.broadcasted_iota(jnp.int32, (pad, D), 0) == 0, 1.0, 0.0
            ).astype(BF)

        pl.semaphore_wait(bar, len(partners))

        mine = pl.ds(pl.multiple_of(l * piece, piece), piece)

        def bias_copy(k):
            return remote(cb1_r, B1.at[t], bs.at[k], br.at[k], (b, (t + k) % nt))

        def along(up, hop, arr, shard):
            src = (w1_h, w2_h)[arr].at[mine] if hop == 1 else (W1, W2)[arr].at[shard, mine]
            step = 1 if up else -1
            return remote(
                src, (W1, W2)[arr].at[shard, mine], zs.at[int(up), hop, arr], zr.at[int(up), hop, arr], (b, t + step)
            )

        def can_send(up, hop):
            return (t - hop + 1 >= 0) & (t + 1 < nt) if up else (t + hop - 1 < nt) & (t >= 1)

        def can_take(up, hop):
            return t - hop >= 0 if up else t + hop < nt

        def send_hop(hop):
            for up in (True, False):
                @pl.when(can_send(up, hop))
                def _():
                    for arr in range(2):
                        along(up, hop, arr, t - hop + 1 if up else t + hop - 1).start()

        def sent_hop(hop):
            for up in (True, False):
                @pl.when(can_send(up, hop))
                def _():
                    for arr in range(2):
                        along(up, hop, arr, t - hop + 1 if up else t + hop - 1).wait_send()

        def take_hop(hop):
            for up in (True, False):
                @pl.when(can_take(up, hop))
                def _():
                    for arr in range(2):
                        shard = t - hop if up else t + hop
                        remote(
                            (W1, W2)[arr].at[shard, mine], (W1, W2)[arr].at[shard, mine],
                            zs.at[int(up), hop, arr], zr.at[int(up), hop, arr], (b, t - 1 if up else t + 1),
                        ).wait_recv()

        for k in range(1, nt):
            bias_copy(k).start()
        send_hop(1)

        def shard_at(k):
            if k == 0:
                return t
            return sum(jnp.where(t == s, near[s][k - 1], 0) for s in range(nt))

        order = [shard_at(k) for k in range(nt)]
        moves = (
            (l, p_first), (l, p_second), (p_first, p_second),
            (l, p_core), (p_first, p_core), (p_second, p_core), (p_both, p_core),
        )

        def plane(k, move):
            who, peer = moves[move]
            part = pl.ds(pl.multiple_of(who * piece, piece), piece)
            return [
                remote(
                    w.at[order[k], part], w.at[order[k], part], ps.at[k, move, arr], pr.at[k, move, arr],
                    (base + peer, t),
                )
                for arr, w in enumerate((W1, W2))
            ]

        def act(k, stage):
            if stage == 0:
                take_hop(k)
                if k + 1 < nt:
                    send_hop(k + 1)
                go = (0, 1)
            elif stage == 1:
                for cp in plane(k, 0):
                    cp.wait_recv()
                go = (2, 3, 4)
            elif stage == 2:
                for move in (1, 2):
                    for cp in plane(k, move):
                        cp.wait_recv()
                go = (5, 6)
            else:
                for move in range(3, 7):
                    for cp in plane(k, move):
                        cp.wait_recv()
                for move in range(7):
                    for cp in plane(k, move):
                        cp.wait_send()
                sent_hop(k)
                if k == 1:
                    for step in range(1, nt):
                        bias_copy(step).wait()
                go = ()
            for move in go:
                for cp in plane(k, move):
                    cp.start()

        plan = {
            (0, 1, 1): [(1, 0)],
            (1, 1, 1): [(1, 1)],
            (1, 1, 2): [(2, 0)],
            (2, 0, 2): [(1, 2)],
            (2, 1, 2): [(2, 1), (3, 0)],
            (3, 0, 2): [(2, 2)],
        }

        def tick(g, section, step):
            for (gg, ss, when), what in plan.items():
                if (gg, ss) == (g, section):
                    @pl.when(step == when)
                    def _():
                        for k, stage in what:
                            act(k, stage)

        def token_forward(g, p, n2x, gpx):
            q = g * pairs + p
            slot = q % SLOTS
            ahead = q + SLOTS - 1

            @pl.when(ahead < nt * pairs)
            def _():
                for cp in fetch(ahead, ahead % SLOTS):
                    cp.start()

            for cp in fetch(q, slot):
                cp.wait()

            grp = (t + 1 + g) % nt
            both_x = xb[slot]
            both_g = gb[slot]
            for e in range(2):
                i = 2 * p + e
                at = pl.multiple_of(i * SP, 16)
                x = both_x[e].astype(F32)
                scaled, _ = normal(x)
                n1 = (scaled * g1_r[...] + b1_r[...]).astype(BF)
                th = dot(w1t[...], n1) + tb1c[...]
                r, _ = gelu_parts(th)
                ta = (th * r).astype(BF)
                u = x + dot(w2t[...], ta) + tb2c[...]
                if g == nt - 1:
                    n1_s[i, 0:S, :] = n1
                    ta_s[i] = ta
                    u_s[i] = u
                scaled, _ = normal(u)
                n2x[pl.ds(at, S), :] = (scaled * g2_r[...] + b2_r[...]).astype(BF)
                valid = jnp.where(own * grp + i < cnt[0], 0.5, 0.0)
                gpx[pl.ds(at, S), :] = (both_g[e].astype(F32) * valid).astype(BF)

        def hidden(rr, n2x, gpx, w1, w2, bias, slot):
            ch = dot(n2x[rr, :], w1) + bias
            da = dot_nt(gpx[rr, :], w2)
            r, s = gelu_parts(ch)
            ca[slot, rr, :] = (ch * r).astype(BF)
            grad = da * slope_twice(r, s)
            return grad, grad.astype(BF)

        def chunk_at(j):
            return pl.ds(pl.multiple_of(j * chunk, 16), chunk)

        def first(p, carry):
            token_forward(0, p, n2a, gpa)
            return carry

        lax.fori_loop(0, pairs, first, 0)
        for cp in local:
            cp.wait()
        dacc[...] = jnp.zeros_like(dacc)

        for g in range(nt):
            n2x, gpx = ((n2a, gpa), (n2b, gpb))[g % 2]
            n2y, gpy = ((n2b, gpb), (n2a, gpa))[g % 2]

            def step(j, carry):
                tick(g, 0, j)
                rr = chunk_at(j)
                grad, dh = hidden(rr, n2x, gpx, W1[t], W2[t], B1[t], 0)
                dch[rr, :] = dh
                gcb1[...] += total_of(grad)
                return carry

            lax.fori_loop(0, n_chunk, step, 0)

            def weights(p, carry):
                tick(g, 1, p)
                if g + 1 < nt:
                    token_forward(g + 1, p, n2y, gpy)
                ks = pl.ds(pl.multiple_of(p * third, third), third)
                acc[1, ks, :] += dot_tn(ca[0, :, ks], gpx[...])
                acc[0, ks, :] += dot_tn(n2x[:, ks], dch[...])
                return carry

            lax.fori_loop(0, pairs, weights, 0)
        n2, gp = ((n2a, gpa), (n2b, gpb))[(nt - 1) % 2]

        half, quarter = D // 2, D // 4
        bit_f = (1 - c) * ((l // 2) % 2) + c * ((l // 4) % 2)
        bit_s = (1 - c) * ((l // 4) % 2) + c * ((l // 2) % 2)

        def span(start, size):
            return pl.ds(pl.multiple_of(start, quarter), size)

        here_f = span(bit_f * half, half)
        there_f = span((1 - bit_f) * half, half)
        here_s = span(bit_f * half + bit_s * quarter, quarter)
        there_s = span(bit_f * half + (1 - bit_s) * quarter, quarter)

        idle_n, idle_g = ((n2b, gpb), (n2a, gpa))[(nt - 1) % 2]
        sends = (idle_n.at[0:D], idle_g.at[0:half], idle_g.at[half : half + quarter])

        def sum_copy(stage):
            if stage < 3:
                src = sends[stage]
                dst = (rcv0, rcv1, rcv2)[stage]
                peer = (p_core, p_first, p_second)[stage]
            else:
                src = (gwb.at[c, here_s], gwb.at[c, here_f], gwb.at[c])[stage - 3]
                dst = src
                peer = (p_second, p_first, p_core)[stage - 3]
            return remote(src, dst, as_.at[stage], ar_.at[stage], (base + peer, t))

        def sum_step(stage):
            if stage > 0:
                sum_copy(stage - 1).wait()
            if stage == 0:
                sends[0][...] = acc[1 - c].astype(BF)
                sum_copy(0).start()
            elif stage == 1:
                sends[1][...] = (acc[c, there_f, :] + rcv0[there_f, :].astype(F32)).astype(BF)
                sum_copy(1).start()
                acc[c, here_f, :] += rcv0[here_f, :].astype(F32)
            elif stage == 2:
                sends[2][...] = (
                    acc[c, there_s, :] + rcv1[span((1 - bit_s) * quarter, quarter), :].astype(F32)
                ).astype(BF)
                sum_copy(2).start()
                acc[c, here_s, :] += rcv1[span(bit_s * quarter, quarter), :].astype(F32)
            elif stage == 3:
                total = acc[c, here_s, :] + rcv2[...].astype(F32)
                for n, e in enumerate(extra):
                    sndx[n] = total.astype(BF)
                    cp = remote(sndx.at[n], rcvx.at[n], axs.at[n], axr.at[n], (flip(b, e), t))
                    cp.start()
                    cp.wait()
                    total = sndx[n].astype(F32) + rcvx[n].astype(F32)
                gwb[c, here_s, :] = total.astype(BF)
                sum_copy(3).start()
            elif stage < 6:
                sum_copy(stage).start()

        sum_step(0)

        late = {2: 1, 7: 2}

        def gather(j, grad):
            for e in range(2):
                dacc[2 * j + e] += grad[e * SP : e * SP + S, :]

        def back(rr, k):
            return dot_nt(dch[rr, :], W1[order[k]])

        for k in range(1, nt - 1):
            def other(j, carry):
                if k == 1:
                    @pl.when(j == 0)
                    def _():
                        act(3, 1)
                        act(1, 3)
                else:
                    @pl.when(j == 0)
                    def _():
                        act(3, 2)
                        act(2, 3)
                for when, stage in late.items():
                    if when // n_chunk == k - 1:
                        @pl.when(j == when % n_chunk)
                        def _():
                            sum_step(stage)
                rr = chunk_at(j)
                gather(j, back(rr, k - 1))
                shard = order[k]
                dch[rr, :] = hidden(rr, n2, gp, W1[shard], W2[shard], B1[shard], k)[1]
                return carry

            lax.fori_loop(0, n_chunk, other, 0)

        def last(j):
            rr = chunk_at(j)
            k = nt - 1
            earlier = back(rr, k - 1)
            shard = order[k]
            dh = hidden(rr, n2, gp, W1[shard], W2[shard], B1[shard], k)[1]
            gather(j, earlier + dot_nt(dh, W1[shard]))

        def xcopy(p, slot):
            at = pl.ds(own * t + 2 * p, 2)
            return pltpu.make_async_copy(img.at[at], xb.at[slot], x_sem.at[slot])

        def gcopy(i):
            return pltpu.make_async_copy(dacc.at[i], gim_h.at[i], i_sem.at[i])

        def token_back(p):
            slot = p
            xcopy(p, slot).wait()
            both_x = xb[slot]
            both = [dacc[2 * p + e] for e in range(2)]
            for e in range(2):
                i = 2 * p + e
                at = pl.multiple_of(i * SP, 16)
                dn2 = both[e]
                g = gp[pl.ds(at, S), :].astype(F32) * 2.0
                scaled, inverse = normal(u_s[i])
                vec[0:1, :] += total_of(dn2 * scaled)
                vec[1:2, :] += total_of(dn2)
                vec[4:5, :] += total_of(g)
                du = g + norm_back(dn2, g2_r[...], scaled, inverse)
                dz = du.astype(BF)
                tb2acc[...] += jnp.sum(dz.astype(F32), axis=1, keepdims=True)
                n1 = n1_s[i]
                sm_r[SP : SP + S, :] += dot_nt(dz, ta_s[i])
                th = dot(w1t[...], n1[0:S, :]) + tb1c[...]
                r, s = gelu_parts(th)
                dth = (dot(tw2_r[...], dz) * slope_twice(r, s)).astype(BF)
                sm_r[0:SP, :] += dot_nt(n1, dth)
                dn1 = dot(tw1_r[...], dth)
                scaled, inverse = normal(both_x[e].astype(F32))
                vec[2:3, :] += total_of(dn1 * scaled)
                vec[3:4, :] += total_of(dn1)
                dacc[i] = du + norm_back(dn1, g1_r[...], scaled, inverse)

        def flush_pair(p):
            for e in range(2):
                gcopy(2 * p + e).start()

        def ocopy(i):
            return pltpu.make_async_copy(outs.at[i], out_h.at[i], o_sem.at[i])

        def flush_result(j):
            for e in range(2):
                ocopy(2 * j + e).start()

        def result(j):
            rr = chunk_at(j)
            total = dot(ca[0, rr, :], W2[t])
            for k in range(1, nt):
                total += dot(ca[k, rr, :], W2[order[k]])
            for e in range(2):
                v = total[e * SP : e * SP + S, :] * 0.5 + u_s[2 * j + e] + cb2_r[...]
                outs[2 * j + e] = v.astype(BF)

        for p in range(pairs):
            xcopy(p, p).start()
        act(3, 3)

        def final(j, carry):
            @pl.when(j == 1)
            def _():
                sum_step(2)

            last(j)
            return carry

        lax.fori_loop(0, n_chunk, final, 0)

        def token(p, carry):
            @pl.when(p == 2)
            def _():
                sum_step(3)

            token_back(p)
            flush_pair(p)
            return carry

        lax.fori_loop(0, pairs, token, 0)

        low = 2 * SP
        sm_r[SP : SP + S, :] = sm_r[SP : SP + S, :] * 0.5
        for k in range(5):
            for h in range(2):
                sm_r[low + 2 * k + h : low + 2 * k + h + 1, :] = vec[k : k + 1, h * HD : (h + 1) * HD]
        sm_r[low + 10 : low + 11, 0:S] = total_of(eye(S, F32) * tb2acc[...])
        for s in range(nt):
            for h in range(2):
                r = low + 11 + 2 * s + h
                sm_r[r : r + 1, :] = jnp.where(t == s, 1.0, 0.0) * gcb1[:, h * HD : (h + 1) * HD]

        part, small = SMALL // RING, SMALL // RING // nt
        s_snd[...] = sm_r[...].astype(BF)

        def eighths(k, back):
            whom = (base + (l + k) % RING, t)
            if back:
                ref = s_all.at[pl.ds(pl.multiple_of(l * part, part), part)]
                return remote(ref, ref, sqs.at[k], sqr.at[k], whom)
            src = s_snd.at[pl.ds(pl.multiple_of(((l + k) % RING) * part, part), part)]
            return remote(src, s_rcv.at[k], sps.at[k], spr.at[k], whom)

        def quarters(k, back):
            whom = (b, (t + k) % nt)
            if back:
                ref = s_all.at[pl.ds(pl.multiple_of(l * part + t * small, small), small)]
                return remote(ref, ref, sys_.at[k], syr.at[k], whom)
            src = z_snd.at[pl.ds(pl.multiple_of(((t + k) % nt) * small, small), small)]
            return remote(src, z_rcv.at[k], szs.at[k], szr.at[k], whom)

        for k in range(1, RING):
            eighths(k, False).start()

        def small_step(stage):
            if stage == 1:
                total = sm_r[pl.ds(pl.multiple_of(l * part, part), part), :]
                for k in range(1, RING):
                    eighths(k, False).wait()
                    total += s_rcv[k].astype(F32)
                s_mid[...] = total
                z_snd[...] = total.astype(BF)
                for k in range(1, nt):
                    quarters(k, False).start()
            elif stage == 2:
                total = s_mid[pl.ds(pl.multiple_of(t * small, small), small), :]
                for k in range(1, nt):
                    quarters(k, False).wait()
                    total += z_rcv[k].astype(F32)
                for n, e in enumerate(extra):
                    x_snd[n] = total.astype(BF)
                    cp = remote(x_snd.at[n], x_rcv.at[n], sxs.at[n], sxr.at[n], (flip(b, e), t))
                    cp.start()
                    cp.wait()
                    total = x_snd[n].astype(F32) + x_rcv[n].astype(F32)
                s_all[pl.ds(pl.multiple_of(l * part + t * small, small), small), :] = total.astype(BF)
                for k in range(1, nt):
                    quarters(k, True).start()
            elif stage == 3:
                for k in range(1, nt):
                    quarters(k, True).wait()
                for k in range(1, RING):
                    eighths(k, True).start()
            else:
                for k in range(1, RING):
                    eighths(k, True).wait()

        def rest(j, carry):
            @pl.when(j == 1)
            def _():
                sum_step(4)

            result(j)
            flush_result(j)
            return carry

        lax.fori_loop(0, n_chunk, rest, 0)
        small_step(1)
        small_step(2)
        sum_step(5)
        small_step(3)
        sum_copy(5).wait()
        flush = pltpu.make_async_copy(gwb, gwb_o, l_sem.at[0])
        flush.start()
        for i in range(own):
            ocopy(i).wait()
            gcopy(i).wait()
        small_step(4)
        flush.wait()

    V = pltpu.VMEM
    DMA = pltpu.SemaphoreType.DMA
    any_ = pl.BlockSpec(memory_space=pl.ANY)
    vm = pl.BlockSpec(memory_space=V)
    f = lambda *shape: jax.ShapeDtypeStruct(shape, F32)
    h = lambda *shape: jax.ShapeDtypeStruct(shape, BF)
    xn = max(1, len(extra))
    part, small = SMALL // RING, SMALL // RING // nt
    raw = pl.pallas_call(
        kernel,
        out_shape=(h(own, S, D), f(own, S, D), h(2, D, D), h(SMALL, DS)),
        in_specs=[any_, any_, any_, any_, vm, pl.BlockSpec(memory_space=pltpu.SMEM)] + [vm] * 9,
        out_specs=(any_, any_, any_, vm),
        scratch_shapes=[
            V((nt, D, H), BF), V((nt, H, D), BF), V((nt, 1, H), F32),
            V((SLOTS, 2, S, D), BF), V((SLOTS, 2, S, D), BF),
            V((rows, D), BF), V((rows, D), BF), V((rows, D), BF), V((rows, D), BF),
            V((nt, rows, H), BF), V((rows, H), BF), V((own, S, D), F32),
            V((own, S, D), F32), V((own, DS, D), BF), V((own, SP, D), BF),
            V((DS, S), BF), V((S, DS), BF), V((DS, S), BF), V((DS, 1), F32), V((S, 1), F32),
            V((1, H), F32), V((8, D), F32), V((S, 1), F32), V((own, S, D), BF),
            V((1, H), F32), V((1, D), F32), V((1, D), F32), V((1, D), F32), V((1, D), F32), V((1, D), F32),
            V((2, D, D), F32), V((SMALL, DS), F32),
            V((D, D), BF), V((D // 2, D), BF), V((D // 4, D), BF),
            V((xn, D // 4, D), BF), V((xn, D // 4, D), BF), V((2, D, D), BF),
            V((SMALL, DS), BF), V((RING, part, DS), BF), V((part, DS), F32), V((part, DS), BF), V((nt, small, DS), BF),
            V((xn, small, DS), BF), V((xn, small, DS), BF),
            DMA((SLOTS,)), DMA((SLOTS,)), DMA((2,)), DMA((own,)), DMA((own,)),
            DMA((2, nt, 2)), DMA((2, nt, 2)), DMA((nt, 7, 2)), DMA((nt, 7, 2)), DMA((nt,)), DMA((nt,)),
            DMA((6,)), DMA((6,)), DMA((xn,)), DMA((xn,)), DMA((RING,)), DMA((RING,)), DMA((nt,)), DMA((nt,)),
            DMA((xn,)), DMA((xn,)), DMA((nt,)), DMA((nt,)), DMA((RING,)), DMA((RING,)),
        ],
        compiler_params=pltpu.CompilerParams(
            collective_id=0, has_side_effects=True, vmem_limit_bytes=65200 * 1024
        ),
    )(
        images, cot, cw1, cw2, cb1, counts,
        g1, b1, g2, b2, tw1, tw2.T, tb1, tb2, cb2,
    )

    def unpack(
        out_r, gim_r, gwb_r, s_all,
        out_o, gim_o, gg1_o, gb1_o, gtw1_o, gtb1_o, gtw2_o, gtb2_o, gg2_o, gb2_o, gw1_o, gcb1_o, gw2_o, gcb2_o,
        w_s, sem,
    ):
        t = lax.axis_index("tensor")
        moves = [
            pltpu.make_async_copy(out_r, out_o, sem.at[0]), pltpu.make_async_copy(gim_r, gim_o, sem.at[1]),
        ]
        for cp in moves:
            cp.start()
        for n, ref in enumerate((gw1_o, gw2_o)):
            w_s[n] = gwb_r[n].astype(F32)
            moves.append(pltpu.make_async_copy(w_s.at[n], ref, sem.at[2 + n]))
            moves[-1].start()
        low = 2 * SP
        gtw1_o[...] = s_all[0:S, :].astype(F32)
        gtw2_o[...] = s_all[SP : SP + S, :].astype(F32)
        ends = s_all[low : low + 32, :].astype(F32)
        at = S // 16 * 16
        gtb1_o[...] = s_all[at : at + 16, :].astype(F32)[S - at]
        gtb2_o[...] = ends[10, 0:S]
        for k, ref in enumerate((gg2_o, gb2_o, gg1_o, gb1_o, gcb2_o)):
            for h in range(2):
                ref[h * HD : (h + 1) * HD] = ends[2 * k + h]
        for h in range(2):
            total = ends[11 + h] * jnp.where(t == 0, 1.0, 0.0)
            for s in range(1, nt):
                total += ends[11 + 2 * s + h] * jnp.where(t == s, 1.0, 0.0)
            gcb1_o[h * HD : (h + 1) * HD] = total
        for cp in moves:
            cp.wait()

    out = pl.pallas_call(
        unpack,
        out_shape=(
            h(own, S, D), f(own, S, D), f(D), f(D), f(S, DS), f(DS), f(S, DS), f(S), f(D), f(D),
            f(D, H), f(H), f(H, D), f(D),
        ),
        in_specs=[any_, any_, vm, vm],
        out_specs=(any_, any_) + (vm,) * 8 + (any_, vm, any_, vm),
        scratch_shapes=[V((2, D, D), F32), DMA((4,))],
        compiler_params=pltpu.CompilerParams(vmem_limit_bytes=40 * 2**20),
    )(*raw)
    return out[:6] + (out[6].T,) + out[7:]


def solution(mesh):
    nb, nt = mesh.shape["batch"], mesh.shape["tensor"]
    in_specs = (
        P("batch", None, None), P("batch"),
        P(), P(), P(), P(), P(), P(), P(), P(),
        P(None, "tensor"), P("tensor"), P("tensor", None), P(),
        P("batch", None, None),
    )
    both = P(("batch", "tensor"), None, None)
    out_specs = (
        both, both,
        P(), P(), P(), P(), P(), P(), P(), P(),
        P(None, "tensor"), P("tensor"), P("tensor", None), P(),
    )
    return jax.shard_map(
        lambda *args: per_device(nb, nt, args),
        mesh=mesh, in_specs=in_specs, out_specs=out_specs, check_vma=False,
    )
```

```python
import jax
import jax.numpy as jnp
from jax import lax
from jax.experimental import pallas as pl
from jax.experimental.pallas import tpu as pltpu
from jax.sharding import PartitionSpec as P

EPSILON = 1e-06
ROOT_HALF = 0.7071067811865476
INV_ROOT_TAU = 0.3989422804014327
LOG2_E = 1.4426950408889634
MESH = pl.DeviceIdType.MESH
BF = jnp.bfloat16
F32 = jnp.float32
SLOTS = 3
RING = 8
SMALL = 512


def dot(a, b):
    return lax.dot_general(a, b, (((1,), (0,)), ((), ())), preferred_element_type=F32)


def dot_nt(a, b):
    return lax.dot_general(a, b, (((1,), (1,)), ((), ())), preferred_element_type=F32)


def dot_tn(a, b):
    return lax.dot_general(a, b, (((0,), (0,)), ((), ())), preferred_element_type=F32)


def flip(v, bit):
    step = 1 << bit
    return v + (1 - 2 * ((v // step) % 2)) * step


def normal(v):
    center = v - jnp.mean(v, axis=-1, keepdims=True)
    inverse = lax.rsqrt(jnp.mean(center * center, axis=-1, keepdims=True) + EPSILON)
    return center * inverse, inverse


def gelu_parts(v):
    s = v * ROOT_HALF
    return 1.0 + lax.erf(s), s


def slope_twice(r, s):
    return r + (s * jnp.exp2(s * s * -LOG2_E)) * (2.0 * INV_ROOT_TAU / ROOT_HALF)


def norm_back(grad, gain, scaled, inverse):
    weighted = grad * gain
    return inverse * (
        weighted
        - jnp.mean(weighted, axis=-1, keepdims=True)
        - scaled * jnp.mean(weighted * scaled, axis=-1, keepdims=True)
    )


def eye(n, dtype, value=1.0):
    rows = lax.broadcasted_iota(jnp.int32, (n, n), 0)
    cols = lax.broadcasted_iota(jnp.int32, (n, n), 1)
    return jnp.where(rows == cols, value, 0.0).astype(dtype)


def column(row):
    n = row.shape[1]
    return jnp.sum(eye(n, F32) * row, axis=1, keepdims=True)


def total_of(v):
    return jnp.sum(v, axis=0, keepdims=True)


def per_device(nb, nt, args):
    (images, counts, g1, b1, tw1, tb1, tw2, tb2, g2, b2, cw1, cb1, cw2, cb2, cot) = args
    slots, S, D = images.shape
    DS = tw1.shape[1]
    H = cw1.shape[1]
    own = slots // nt
    SP = -(-S // 16) * 16
    pairs = own // 2
    rows = own * SP
    chunk = 2 * SP
    n_chunk = rows // chunk
    third = D // pairs
    piece = D // RING
    HD = D // 2
    near = [sorted((s for s in range(nt) if s != t), key=lambda s: (abs(s - t), s)) for t in range(nt)]
    if nt == 4:
        near[2] = [3, 1, 0]
    extra = range(3, nb.bit_length() - 1)

    def kernel(
        img, cot_h, w1_h, w2_h, cb1_1, cnt, g1_1, b1_1, g2_1, b2_1, tw1_r, w2t_r, tb1_1, tb2_1, cb2_1,
        out_h, gim_h, gwb_o, s_all,
        W1, W2, B1, xb, gb, n2a, n2b, gpa, gpb, ca, dch, dacc, u_s, ta_s, n1_s, w1t, w2t, tw2_r, tb1c, tb2c,
        gcb1, vec, tb2acc, outs,
        cb1_r, g1_r, b1_r, g2_r, b2_r, cb2_r, acc, sm_r, rcv0, rcv1, rcv2, rcvx, gwb,
        s_snd, s_rcv, z_rcv, x_snd, x_rcv,
        x_sem, g_sem, l_sem, o_sem, i_sem, zs, zr, ps, pr, bs, br,
        as_, ar_, axs, axr, sps, spr, szs, szr, sxs, sxr, sqs, sqr,
    ):
        b = lax.axis_index("batch")
        t = lax.axis_index("tensor")
        l = b % RING
        base = b - l
        c = l % 2
        lf, ls = flip(l, 1), flip(l, 2)
        p_first = (1 - c) * lf + c * ls
        p_second = (1 - c) * ls + c * lf
        p_both = flip(flip(l, 1), 2)
        p_core = flip(l, 0)

        def remote(src, dst, ss, rs, dev):
            return pltpu.make_async_remote_copy(src, dst, ss, rs, device_id=dev, device_id_type=MESH)

        bar = pltpu.get_barrier_semaphore()
        partners = [(b, (t + k) % nt) for k in range(1, nt)]
        partners += [(base + (l + k) % RING, t) for k in range(1, RING)]
        partners += [(flip(b, e), t) for e in extra]
        for d in partners:
            pl.semaphore_signal(bar, inc=1, device_id=d, device_id_type=MESH)

        def fetch(q, slot):
            grp = (t + 1 + q // pairs) % nt
            at = pl.ds(own * grp + 2 * (q % pairs), 2)
            return (
                pltpu.make_async_copy(img.at[:, at, :], xb.at[slot], x_sem.at[slot]),
                pltpu.make_async_copy(cot_h.at[:, at, :], gb.at[slot], g_sem.at[slot]),
            )

        for q in range(SLOTS - 1):
            for cp in fetch(q, q):
                cp.start()
        local = [
            pltpu.make_async_copy(w1_h, W1.at[t], l_sem.at[0]),
            pltpu.make_async_copy(w2_h, W2.at[t], l_sem.at[1]),
        ]
        for cp in local:
            cp.start()

        cb1_r[...] = cb1_1[...].reshape(1, H)
        for ref, one in ((g1_r, g1_1), (b1_r, b1_1), (g2_r, g2_1), (b2_r, b2_1), (cb2_r, cb2_1)):
            ref[...] = one[...].reshape(1, D)
        B1[t] = cb1_r[...]
        w1t[...] = dot_nt(eye(DS, BF), tw1_r[...]).astype(BF)
        w2t[...] = (w2t_r[...].astype(F32) * 0.5).astype(BF)
        tw2_r[...] = dot_nt(eye(DS, BF), w2t[...]).astype(BF)
        tb1c[...] = column(tb1_1[...].reshape(1, DS))
        tb2c[...] = column(tb2_1[...].reshape(1, S))
        acc[...] = jnp.zeros_like(acc)
        gcb1[...] = jnp.zeros_like(gcb1)
        vec[...] = jnp.zeros_like(vec)
        tb2acc[...] = jnp.zeros_like(tb2acc)
        sm_r[...] = jnp.zeros_like(sm_r)
        pad = SP - S
        for i in range(own):
            for ref in (n2a, n2b, gpa, gpb):
                ref[i * SP + S : (i + 1) * SP, :] = jnp.zeros((pad, D), BF)
            n1_s[i, S:SP, :] = jnp.where(
                lax.broadcasted_iota(jnp.int32, (pad, D), 0) == 0, 1.0, 0.0
            ).astype(BF)

        pl.semaphore_wait(bar, len(partners))

        mine = pl.ds(pl.multiple_of(l * piece, piece), piece)

        def bias_copy(k):
            return remote(cb1_r, B1.at[t], bs.at[k], br.at[k], (b, (t + k) % nt))

        def along(up, hop, arr, shard):
            src = (w1_h, w2_h)[arr].at[mine] if hop == 1 else (W1, W2)[arr].at[shard, mine]
            step = 1 if up else -1
            return remote(
                src, (W1, W2)[arr].at[shard, mine], zs.at[int(up), hop, arr], zr.at[int(up), hop, arr], (b, t + step)
            )

        def can_send(up, hop):
            return (t - hop + 1 >= 0) & (t + 1 < nt) if up else (t + hop - 1 < nt) & (t >= 1)

        def can_take(up, hop):
            return t - hop >= 0 if up else t + hop < nt

        def send_hop(hop):
            for up in (True, False):
                @pl.when(can_send(up, hop))
                def _():
                    for arr in range(2):
                        along(up, hop, arr, t - hop + 1 if up else t + hop - 1).start()

        def sent_hop(hop):
            for up in (True, False):
                @pl.when(can_send(up, hop))
                def _():
                    for arr in range(2):
                        along(up, hop, arr, t - hop + 1 if up else t + hop - 1).wait_send()

        def take_hop(hop):
            for up in (True, False):
                @pl.when(can_take(up, hop))
                def _():
                    for arr in range(2):
                        shard = t - hop if up else t + hop
                        remote(
                            (W1, W2)[arr].at[shard, mine], (W1, W2)[arr].at[shard, mine],
                            zs.at[int(up), hop, arr], zr.at[int(up), hop, arr], (b, t - 1 if up else t + 1),
                        ).wait_recv()

        for k in range(1, nt):
            bias_copy(k).start()
        send_hop(1)

        def shard_at(k):
            if k == 0:
                return t
            return sum(jnp.where(t == s, near[s][k - 1], 0) for s in range(nt))

        order = [shard_at(k) for k in range(nt)]
        moves = (
            (l, p_first), (l, p_second), (p_first, p_second),
            (l, p_core), (p_first, p_core), (p_second, p_core), (p_both, p_core),
        )

        def plane(k, move):
            who, peer = moves[move]
            part = pl.ds(pl.multiple_of(who * piece, piece), piece)
            return [
                remote(
                    w.at[order[k], part], w.at[order[k], part], ps.at[k, move, arr], pr.at[k, move, arr],
                    (base + peer, t),
                )
                for arr, w in enumerate((W1, W2))
            ]

        def act(k, stage):
            if stage == 0:
                take_hop(k)
                if k + 1 < nt:
                    send_hop(k + 1)
                go = (0, 1)
            elif stage == 1:
                for cp in plane(k, 0):
                    cp.wait_recv()
                go = (2, 3, 4)
            elif stage == 2:
                for move in (1, 2):
                    for cp in plane(k, move):
                        cp.wait_recv()
                go = (5, 6)
            else:
                for move in range(3, 7):
                    for cp in plane(k, move):
                        cp.wait_recv()
                for move in range(7):
                    for cp in plane(k, move):
                        cp.wait_send()
                sent_hop(k)
                if k == 1:
                    for step in range(1, nt):
                        bias_copy(step).wait()
                go = ()
            for move in go:
                for cp in plane(k, move):
                    cp.start()

        plan = {
            (0, 1, 0): [(1, 0)],
            (1, 0, 1): [(1, 1), (2, 0)],
            (1, 1, 1): [(1, 2)],
            (2, 0, 0): [(2, 1), (3, 0)],
            (2, 1, 1): [(2, 2)],
            (2, 1, 2): [(3, 1)],
            (3, 1, 0): [(3, 2)],
        }

        def tick(g, section, step):
            for (gg, ss, when), what in plan.items():
                if (gg, ss) == (g, section):
                    @pl.when(step == when)
                    def _():
                        for k, stage in what:
                            act(k, stage)

        def token_forward(g, p, n2x, gpx):
            q = g * pairs + p
            slot = q % SLOTS
            ahead = q + SLOTS - 1

            @pl.when(ahead < nt * pairs)
            def _():
                for cp in fetch(ahead, ahead % SLOTS):
                    cp.start()

            for cp in fetch(q, slot):
                cp.wait()

            grp = (t + 1 + g) % nt
            both_x = xb[slot]
            both_g = jnp.swapaxes(gb[slot], 0, 1)
            for e in range(2):
                i = 2 * p + e
                at = pl.multiple_of(i * SP, 16)
                x = both_x[:, e, :].astype(F32)
                scaled, _ = normal(x)
                n1 = (scaled * g1_r[...] + b1_r[...]).astype(BF)
                th = dot(w1t[...], n1) + tb1c[...]
                r, _ = gelu_parts(th)
                ta = (th * r).astype(BF)
                u = x + dot(w2t[...], ta) + tb2c[...]
                if g == nt - 1:
                    n1_s[i, 0:S, :] = n1
                    ta_s[i] = ta
                    u_s[i] = u
                scaled, _ = normal(u)
                n2x[pl.ds(at, S), :] = (scaled * g2_r[...] + b2_r[...]).astype(BF)
                valid = jnp.where(own * grp + i < cnt[0], 0.5, 0.0)
                gpx[pl.ds(at, S), :] = (both_g[e].astype(F32) * valid).astype(BF)

        def hidden(rr, n2x, gpx, w1, w2, bias, slot):
            ch = dot(n2x[rr, :], w1) + bias
            da = dot_nt(gpx[rr, :], w2)
            r, s = gelu_parts(ch)
            ca[slot, rr, :] = (ch * r).astype(BF)
            grad = da * slope_twice(r, s)
            return grad, grad.astype(BF)

        def chunk_at(j):
            return pl.ds(pl.multiple_of(j * chunk, 16), chunk)

        def first(p, carry):
            token_forward(0, p, n2a, gpa)
            return carry

        lax.fori_loop(0, pairs, first, 0)
        for cp in local:
            cp.wait()
        dacc[...] = jnp.zeros_like(dacc)

        for g in range(nt):
            n2x, gpx = ((n2a, gpa), (n2b, gpb))[g % 2]
            n2y, gpy = ((n2b, gpb), (n2a, gpa))[g % 2]

            def step(j, carry):
                tick(g, 0, j)
                rr = chunk_at(j)
                grad, dh = hidden(rr, n2x, gpx, W1[t], W2[t], B1[t], 0)
                dch[rr, :] = dh
                gcb1[...] += total_of(grad)
                return carry

            lax.fori_loop(0, n_chunk, step, 0)

            def weights(p, carry):
                tick(g, 1, p)
                if g + 1 < nt:
                    token_forward(g + 1, p, n2y, gpy)
                ks = pl.ds(pl.multiple_of(p * third, third), third)
                acc[1, ks, :] += dot_tn(ca[0, :, ks], gpx[...])
                acc[0, ks, :] += dot_tn(n2x[:, ks], dch[...])
                return carry

            lax.fori_loop(0, pairs, weights, 0)
        n2, gp = ((n2a, gpa), (n2b, gpb))[(nt - 1) % 2]

        half, quarter = D // 2, D // 4
        bit_f = (1 - c) * ((l // 2) % 2) + c * ((l // 4) % 2)
        bit_s = (1 - c) * ((l // 4) % 2) + c * ((l // 2) % 2)

        def span(start, size):
            return pl.ds(pl.multiple_of(start, quarter), size)

        here_f = span(bit_f * half, half)
        there_f = span((1 - bit_f) * half, half)
        here_s = span(bit_f * half + bit_s * quarter, quarter)
        there_s = span(bit_f * half + (1 - bit_s) * quarter, quarter)

        idle_n, idle_g = ((n2b, gpb), (n2a, gpa))[(nt - 1) % 2]
        sends = (idle_n.at[0:D], idle_g.at[0:half], idle_g.at[half : half + quarter])

        def sum_copy(stage):
            if stage < 3:
                src = sends[stage]
                dst = (rcv0, rcv1, rcv2)[stage]
                peer = (p_core, p_first, p_second)[stage]
            else:
                src = (gwb.at[c, here_s], gwb.at[c, here_f], gwb.at[c])[stage - 3]
                dst = src
                peer = (p_second, p_first, p_core)[stage - 3]
            return remote(src, dst, as_.at[stage], ar_.at[stage], (base + peer, t))

        def sum_step(stage):
            if stage > 0:
                sum_copy(stage - 1).wait()
            if stage == 0:
                sends[0][...] = acc[1 - c].astype(BF)
                sum_copy(0).start()
            elif stage == 1:
                sends[1][...] = (acc[c, there_f, :] + rcv0[there_f, :].astype(F32)).astype(BF)
                sum_copy(1).start()
                acc[c, here_f, :] += rcv0[here_f, :].astype(F32)
            elif stage == 2:
                sends[2][...] = (
                    acc[c, there_s, :] + rcv1[span((1 - bit_s) * quarter, quarter), :].astype(F32)
                ).astype(BF)
                sum_copy(2).start()
                acc[c, here_s, :] += rcv1[span(bit_s * quarter, quarter), :].astype(F32)
            elif stage == 3:
                total = acc[c, here_s, :] + rcv2[...].astype(F32)
                for n, e in enumerate(extra):
                    spare = idle_g.at[span(half + (n + 1) * quarter, quarter)]
                    spare[...] = total.astype(BF)
                    cp = remote(spare, rcvx.at[n], axs.at[n], axr.at[n], (flip(b, e), t))
                    cp.start()
                    cp.wait()
                    total = spare[...].astype(F32) + rcvx[n].astype(F32)
                gwb[c, here_s, :] = total.astype(BF)
                sum_copy(3).start()
            elif stage < 6:
                sum_copy(stage).start()

        sum_step(0)

        late = {2: 1, 7: 2}

        def gather(j, grad):
            for e in range(2):
                dacc[2 * j + e] += grad[e * SP : e * SP + S, :]

        def back(rr, k):
            return dot_nt(dch[rr, :], W1[order[k]])

        for k in range(1, nt - 1):
            def other(j, carry):
                if k == 1:
                    @pl.when(j == 0)
                    def _():
                        act(1, 3)
                else:
                    @pl.when(j == 0)
                    def _():
                        act(2, 3)
                for when, stage in late.items():
                    if when // n_chunk == k - 1:
                        @pl.when(j == when % n_chunk)
                        def _():
                            sum_step(stage)
                rr = chunk_at(j)
                gather(j, back(rr, k - 1))
                shard = order[k]
                dch[rr, :] = hidden(rr, n2, gp, W1[shard], W2[shard], B1[shard], k)[1]
                return carry

            lax.fori_loop(0, n_chunk, other, 0)

        def last(j):
            rr = chunk_at(j)
            k = nt - 1
            earlier = back(rr, k - 1)
            shard = order[k]
            dh = hidden(rr, n2, gp, W1[shard], W2[shard], B1[shard], k)[1]
            gather(j, earlier + dot_nt(dh, W1[shard]))

        def xcopy(p, slot):
            at = pl.ds(own * t + 2 * p, 2)
            return pltpu.make_async_copy(img.at[:, at, :], xb.at[slot], x_sem.at[slot])

        def gcopy(i):
            return pltpu.make_async_copy(dacc.at[i], gim_h.at[i], i_sem.at[i])

        def token_back(p):
            slot = p
            xcopy(p, slot).wait()
            both_x = xb[slot]
            both = [dacc[2 * p + e] for e in range(2)]
            for e in range(2):
                i = 2 * p + e
                at = pl.multiple_of(i * SP, 16)
                dn2 = both[e]
                g = gp[pl.ds(at, S), :].astype(F32) * 2.0
                scaled, inverse = normal(u_s[i])
                vec[0:1, :] += total_of(dn2 * scaled)
                vec[1:2, :] += total_of(dn2)
                vec[4:5, :] += total_of(g)
                du = g + norm_back(dn2, g2_r[...], scaled, inverse)
                dz = du.astype(BF)
                tb2acc[...] += jnp.sum(dz.astype(F32), axis=1, keepdims=True)
                n1 = n1_s[i]
                sm_r[SP : SP + S, :] += dot_nt(dz, ta_s[i])
                th = dot(w1t[...], n1[0:S, :]) + tb1c[...]
                r, s = gelu_parts(th)
                dth = (dot(tw2_r[...], dz) * slope_twice(r, s)).astype(BF)
                sm_r[0:SP, :] += dot_nt(n1, dth)
                dn1 = dot(tw1_r[...], dth)
                scaled, inverse = normal(both_x[:, e, :].astype(F32))
                vec[2:3, :] += total_of(dn1 * scaled)
                vec[3:4, :] += total_of(dn1)
                dacc[i] = du + norm_back(dn1, g1_r[...], scaled, inverse)

        def flush_pair(p):
            for e in range(2):
                gcopy(2 * p + e).start()

        def ocopy(i):
            return pltpu.make_async_copy(outs.at[i], out_h.at[i], o_sem.at[i])

        def flush_result(j):
            for e in range(2):
                ocopy(2 * j + e).start()

        def result(j):
            rr = chunk_at(j)
            total = dot(ca[0, rr, :], W2[t])
            for k in range(1, nt):
                total += dot(ca[k, rr, :], W2[order[k]])
            for e in range(2):
                v = total[e * SP : e * SP + S, :] * 0.5 + u_s[2 * j + e] + cb2_r[...]
                outs[2 * j + e] = v.astype(BF)

        for p in range(pairs):
            xcopy(p, p).start()
        act(3, 3)

        def final(j, carry):
            @pl.when(j == 1)
            def _():
                sum_step(2)

            last(j)
            return carry

        lax.fori_loop(0, n_chunk, final, 0)

        def token(p, carry):
            @pl.when(p == 0)
            def _():
                sum_step(3)

            @pl.when(p == 2)
            def _():
                sum_step(4)

            token_back(p)
            flush_pair(p)
            return carry

        lax.fori_loop(0, pairs, token, 0)

        low = 2 * SP
        sm_r[SP : SP + S, :] = sm_r[SP : SP + S, :] * 0.5
        for k in range(5):
            for h in range(2):
                sm_r[low + 2 * k + h : low + 2 * k + h + 1, :] = vec[k : k + 1, h * HD : (h + 1) * HD]
        sm_r[low + 10 : low + 11, 0:S] = total_of(eye(S, F32) * tb2acc[...])
        for s in range(nt):
            for h in range(2):
                r = low + 11 + 2 * s + h
                sm_r[r : r + 1, :] = jnp.where(t == s, 1.0, 0.0) * gcb1[:, h * HD : (h + 1) * HD]

        part = SMALL // RING
        s_snd[...] = sm_r[...].astype(BF)

        def eighths(k, back):
            whom = (base + (l + k) % RING, t)
            if back:
                ref = s_all.at[pl.ds(pl.multiple_of(l * part, part), part)]
                return remote(ref, ref, sqs.at[k], sqr.at[k], whom)
            src = s_snd.at[pl.ds(pl.multiple_of(((l + k) % RING) * part, part), part)]
            return remote(src, s_rcv.at[k], sps.at[k], spr.at[k], whom)

        def across(k):
            return remote(z_rcv.at[t], z_rcv.at[t], szs.at[k], szr.at[k], (b, (t + k) % nt))

        for k in range(1, RING):
            eighths(k, False).start()

        def small_step(stage):
            if stage == 1:
                total = sm_r[pl.ds(pl.multiple_of(l * part, part), part), :]
                for k in range(1, RING):
                    eighths(k, False).wait()
                    total += s_rcv[k].astype(F32)
                z_rcv[t] = total.astype(BF)
                for k in range(1, nt):
                    across(k).start()
            elif stage == 2:
                for k in range(1, nt):
                    across(k).wait()
                total = z_rcv[0].astype(F32)
                for s in range(1, nt):
                    total += z_rcv[s].astype(F32)
                for n, e in enumerate(extra):
                    x_snd[n] = total.astype(BF)
                    cp = remote(x_snd.at[n], x_rcv.at[n], sxs.at[n], sxr.at[n], (flip(b, e), t))
                    cp.start()
                    cp.wait()
                    total = x_snd[n].astype(F32) + x_rcv[n].astype(F32)
                s_all[pl.ds(pl.multiple_of(l * part, part), part), :] = total.astype(BF)
                for k in range(1, RING):
                    eighths(k, True).start()
            else:
                for k in range(1, RING):
                    eighths(k, True).wait()

        def rest(j, carry):
            @pl.when(j == 2)
            def _():
                sum_step(5)
                small_step(1)

            result(j)
            flush_result(j)
            return carry

        lax.fori_loop(0, n_chunk, rest, 0)
        small_step(2)
        sum_copy(5).wait()
        flush = pltpu.make_async_copy(gwb, gwb_o, l_sem.at[0])
        flush.start()
        for i in range(own):
            ocopy(i).wait()
            gcopy(i).wait()
        small_step(3)
        flush.wait()

    V = pltpu.VMEM
    DMA = pltpu.SemaphoreType.DMA
    any_ = pl.BlockSpec(memory_space=pl.ANY)
    vm = pl.BlockSpec(memory_space=V)
    f = lambda *shape: jax.ShapeDtypeStruct(shape, F32)
    h = lambda *shape: jax.ShapeDtypeStruct(shape, BF)
    xn = max(1, len(extra))
    part = SMALL // RING
    raw = pl.pallas_call(
        kernel,
        out_shape=(h(own, S, D), f(own, S, D), h(2, D, D), h(SMALL, DS)),
        in_specs=[any_, any_, any_, any_, vm, pl.BlockSpec(memory_space=pltpu.SMEM)] + [vm] * 9,
        out_specs=(any_, any_, any_, vm),
        scratch_shapes=[
            V((nt, D, H), BF), V((nt, H, D), BF), V((nt, 1, H), F32),
            V((SLOTS, S, 2, D), BF), V((SLOTS, S, 2, D), BF),
            V((rows, D), BF), V((rows, D), BF), V((rows, D), BF), V((rows, D), BF),
            V((nt, rows, H), BF), V((rows, H), BF), V((own, S, D), F32),
            V((own, S, D), F32), V((own, DS, D), BF), V((own, SP, D), BF),
            V((DS, S), BF), V((S, DS), BF), V((DS, S), BF), V((DS, 1), F32), V((S, 1), F32),
            V((1, H), F32), V((8, D), F32), V((S, 1), F32), V((own, S, D), BF),
            V((1, H), F32), V((1, D), F32), V((1, D), F32), V((1, D), F32), V((1, D), F32), V((1, D), F32),
            V((2, D, D), F32), V((SMALL, DS), F32),
            V((D, D), BF), V((D // 2, D), BF), V((D // 4, D), BF),
            V((xn, D // 4, D), BF), V((2, D, D), BF),
            V((SMALL, DS), BF), V((RING, part, DS), BF), V((nt, part, DS), BF),
            V((xn, part, DS), BF), V((xn, part, DS), BF),
            DMA((SLOTS,)), DMA((SLOTS,)), DMA((2,)), DMA((own,)), DMA((own,)),
            DMA((2, nt, 2)), DMA((2, nt, 2)), DMA((nt, 7, 2)), DMA((nt, 7, 2)), DMA((nt,)), DMA((nt,)),
            DMA((6,)), DMA((6,)), DMA((xn,)), DMA((xn,)), DMA((RING,)), DMA((RING,)), DMA((nt,)), DMA((nt,)),
            DMA((xn,)), DMA((xn,)), DMA((RING,)), DMA((RING,)),
        ],
        compiler_params=pltpu.CompilerParams(
            collective_id=0, has_side_effects=True, vmem_limit_bytes=65200 * 1024
        ),
    )(
        jnp.swapaxes(images, 0, 1), jnp.swapaxes(cot, 0, 1), cw1, cw2, cb1, counts,
        g1, b1, g2, b2, tw1, tw2.T, tb1, tb2, cb2,
    )

    def unpack(
        out_r, gim_r, gwb_r, s_all,
        out_o, gim_o, gg1_o, gb1_o, gtw1_o, gtb1_o, gtw2_o, gtb2_o, gg2_o, gb2_o, gw1_o, gcb1_o, gw2_o, gcb2_o,
        o_s, m_s, b_s, w_s, sem_in, sem,
    ):
        t = lax.axis_index("tensor")
        cuts = [(gwb_r.at[n], b_s.at[n]) for n in range(2)]
        cuts += [(gim_r.at[i], m_s.at[i]) for i in range(own)]
        cuts += [(out_r.at[i], o_s.at[i]) for i in range(own)]
        goals = [gw1_o, gw2_o] + [gim_o.at[i] for i in range(own)] + [out_o.at[i] for i in range(own)]
        loads = [pltpu.make_async_copy(src, dst, sem_in.at[n]) for n, (src, dst) in enumerate(cuts)]
        for cp in loads:
            cp.start()
        moves = []
        for n, ref in enumerate(goals):
            loads[n].wait()
            src = cuts[n][1]
            if n < 2:
                w_s[n] = b_s[n].astype(F32)
                src = w_s.at[n]
            moves.append(pltpu.make_async_copy(src, ref, sem.at[n]))
            moves[-1].start()
        low = 2 * SP
        gtw1_o[...] = s_all[0:S, :].astype(F32)
        gtw2_o[...] = s_all[SP : SP + S, :].astype(F32)
        ends = s_all[low : low + 32, :].astype(F32)
        at = S // 16 * 16
        gtb1_o[...] = s_all[at : at + 16, :].astype(F32)[S - at]
        gtb2_o[...] = ends[10, 0:S]
        for k, ref in enumerate((gg2_o, gb2_o, gg1_o, gb1_o, gcb2_o)):
            for h in range(2):
                ref[h * HD : (h + 1) * HD] = ends[2 * k + h]
        for h in range(2):
            total = ends[11 + h] * jnp.where(t == 0, 1.0, 0.0)
            for s in range(1, nt):
                total += ends[11 + 2 * s + h] * jnp.where(t == s, 1.0, 0.0)
            gcb1_o[h * HD : (h + 1) * HD] = total
        for cp in moves:
            cp.wait()

    out = pl.pallas_call(
        unpack,
        out_shape=(
            h(own, S, D), f(own, S, D), f(D), f(D), f(S, DS), f(DS), f(S, DS), f(S), f(D), f(D),
            f(D, H), f(H), f(H, D), f(D),
        ),
        in_specs=[any_, any_, any_, vm],
        out_specs=(any_, any_) + (vm,) * 8 + (any_, vm, any_, vm),
        scratch_shapes=[
            V((own, S, D), BF), V((own, S, D), F32), V((2, D, D), BF), V((2, D, D), F32),
            DMA((2 + 2 * own,)), DMA((2 + 2 * own,)),
        ],
        compiler_params=pltpu.CompilerParams(vmem_limit_bytes=65200 * 1024),
    )(*raw)
    return out[:6] + (out[6].T,) + out[7:]


def solution(mesh):
    nb, nt = mesh.shape["batch"], mesh.shape["tensor"]
    in_specs = (
        P("batch", None, None), P("batch"),
        P(), P(), P(), P(), P(), P(), P(), P(),
        P(None, "tensor"), P("tensor"), P("tensor", None), P(),
        P("batch", None, None),
    )
    both = P(("batch", "tensor"), None, None)
    out_specs = (
        both, both,
        P(), P(), P(), P(), P(), P(), P(), P(),
        P(None, "tensor"), P("tensor"), P("tensor", None), P(),
    )
    return jax.shard_map(
        lambda *args: per_device(nb, nt, args),
        mesh=mesh, in_specs=in_specs, out_specs=out_specs, check_vma=False,
    )
```

```python
import jax
import jax.numpy as jnp
from jax import lax
from jax.experimental import pallas as pl
from jax.experimental.pallas import tpu as pltpu
from jax.sharding import PartitionSpec as P

EPSILON = 1e-06
ROOT_HALF = 0.7071067811865476
INV_ROOT_TAU = 0.3989422804014327
LOG2_E = 1.4426950408889634
MESH = pl.DeviceIdType.MESH
BF = jnp.bfloat16
F32 = jnp.float32
SLOTS = 3
RING = 8
SMALL = 512


def dot(a, b):
    return lax.dot_general(a, b, (((1,), (0,)), ((), ())), preferred_element_type=F32)


def dot_nt(a, b):
    return lax.dot_general(a, b, (((1,), (1,)), ((), ())), preferred_element_type=F32)


def dot_tn(a, b):
    return lax.dot_general(a, b, (((0,), (0,)), ((), ())), preferred_element_type=F32)


def flip(v, bit):
    step = 1 << bit
    return v + (1 - 2 * ((v // step) % 2)) * step


def normal(v):
    center = v - jnp.mean(v, axis=-1, keepdims=True)
    inverse = lax.rsqrt(jnp.mean(center * center, axis=-1, keepdims=True) + EPSILON)
    return center * inverse, inverse


def gelu_parts(v):
    s = v * ROOT_HALF
    return 1.0 + lax.erf(s), s


def slope_twice(r, s):
    return r + (s * jnp.exp2(s * s * -LOG2_E)) * (2.0 * INV_ROOT_TAU / ROOT_HALF)


def norm_back(grad, gain, scaled, inverse):
    weighted = grad * gain
    return inverse * (
        weighted
        - jnp.mean(weighted, axis=-1, keepdims=True)
        - scaled * jnp.mean(weighted * scaled, axis=-1, keepdims=True)
    )


def eye(n, dtype, value=1.0):
    rows = lax.broadcasted_iota(jnp.int32, (n, n), 0)
    cols = lax.broadcasted_iota(jnp.int32, (n, n), 1)
    return jnp.where(rows == cols, value, 0.0).astype(dtype)


def column(row):
    n = row.shape[1]
    return jnp.sum(eye(n, F32) * row, axis=1, keepdims=True)


def total_of(v):
    return jnp.sum(v, axis=0, keepdims=True)


def per_device(nb, nt, args):
    (images, counts, g1, b1, tw1, tb1, tw2, tb2, g2, b2, cw1, cb1, cw2, cb2, cot) = args
    slots, S, D = images.shape
    DS = tw1.shape[1]
    H = cw1.shape[1]
    own = slots // nt
    SP = -(-S // 16) * 16
    pairs = own // 2
    rows = own * SP
    chunk = 2 * SP
    n_chunk = rows // chunk
    third = D // pairs
    piece = D // RING
    HD = D // 2
    near = [sorted((s for s in range(nt) if s != t), key=lambda s: (abs(s - t), s)) for t in range(nt)]
    if nt == 4:
        near[2] = [3, 1, 0]
    extra = range(3, nb.bit_length() - 1)

    def kernel(
        img, cot_h, w1_h, w2_h, cb1_1, cnt, g1_1, b1_1, g2_1, b2_1, tw1_r, w2t_r, tb1_1, tb2_1, cb2_1,
        out_h, gim_h, gwb_o, s_all,
        W1, W2, B1, xb, gb, n2a, n2b, gpa, gpb, ca, dch, dacc, u_s, ta_s, n1_s, w1t, w2t, tw2_r, tb1c, tb2c,
        gcb1, vec, tb2acc, outs,
        cb1_r, g1_r, b1_r, g2_r, b2_r, cb2_r, acc, sm_r, rcv0, rcv1, rcv2, rcvx, gwb,
        s_snd, s_rcv, z_rcv, x_snd, x_rcv,
        x_sem, g_sem, l_sem, o_sem, i_sem, zs, zr, ps, pr, bs, br,
        as_, ar_, axs, axr, sps, spr, szs, szr, sxs, sxr, sqs, sqr,
    ):
        b = lax.axis_index("batch")
        t = lax.axis_index("tensor")
        l = b % RING
        base = b - l
        c = l % 2
        lf, ls = flip(l, 1), flip(l, 2)
        p_first = (1 - c) * lf + c * ls
        p_second = (1 - c) * ls + c * lf
        p_both = flip(flip(l, 1), 2)
        p_core = flip(l, 0)

        def remote(src, dst, ss, rs, dev):
            return pltpu.make_async_remote_copy(src, dst, ss, rs, device_id=dev, device_id_type=MESH)

        bar = pltpu.get_barrier_semaphore()
        partners = [(b, (t + k) % nt) for k in range(1, nt)]
        partners += [(base + (l + k) % RING, t) for k in range(1, RING)]
        partners += [(flip(b, e), t) for e in extra]
        for d in partners:
            pl.semaphore_signal(bar, inc=1, device_id=d, device_id_type=MESH)

        def fetch(q, slot):
            grp = (t + 1 + q // pairs) % nt
            at = pl.ds(own * grp + 2 * (q % pairs), 2)
            return (
                pltpu.make_async_copy(img.at[:, at, :], xb.at[slot], x_sem.at[slot]),
                pltpu.make_async_copy(cot_h.at[:, at, :], gb.at[slot], g_sem.at[slot]),
            )

        for q in range(SLOTS - 1):
            for cp in fetch(q, q):
                cp.start()
        local = [
            pltpu.make_async_copy(w1_h, W1.at[t], l_sem.at[0]),
            pltpu.make_async_copy(w2_h, W2.at[t], l_sem.at[1]),
        ]
        for cp in local:
            cp.start()

        cb1_r[...] = cb1_1[...].reshape(1, H)
        for ref, one in ((g1_r, g1_1), (b1_r, b1_1), (g2_r, g2_1), (b2_r, b2_1), (cb2_r, cb2_1)):
            ref[...] = one[...].reshape(1, D)
        B1[t] = cb1_r[...]
        w1t[...] = dot_nt(eye(DS, BF), tw1_r[...]).astype(BF)
        w2t[...] = (w2t_r[...].astype(F32) * 0.5).astype(BF)
        tw2_r[...] = dot_nt(eye(DS, BF), w2t[...]).astype(BF)
        tb1c[...] = column(tb1_1[...].reshape(1, DS))
        tb2c[...] = column(tb2_1[...].reshape(1, S))
        acc[...] = jnp.zeros_like(acc)
        gcb1[...] = jnp.zeros_like(gcb1)
        vec[...] = jnp.zeros_like(vec)
        tb2acc[...] = jnp.zeros_like(tb2acc)
        sm_r[...] = jnp.zeros_like(sm_r)
        pad = SP - S
        for i in range(own):
            for ref in (n2a, n2b, gpa, gpb):
                ref[i * SP + S : (i + 1) * SP, :] = jnp.zeros((pad, D), BF)
            n1_s[i, S:SP, :] = jnp.where(
                lax.broadcasted_iota(jnp.int32, (pad, D), 0) == 0, 1.0, 0.0
            ).astype(BF)

        pl.semaphore_wait(bar, len(partners))

        mine = pl.ds(pl.multiple_of(l * piece, piece), piece)

        def bias_copy(k):
            return remote(cb1_r, B1.at[t], bs.at[k], br.at[k], (b, (t + k) % nt))

        def along(up, hop, arr, shard):
            src = (w1_h, w2_h)[arr].at[mine] if hop == 1 else (W1, W2)[arr].at[shard, mine]
            step = 1 if up else -1
            return remote(
                src, (W1, W2)[arr].at[shard, mine], zs.at[int(up), hop, arr], zr.at[int(up), hop, arr], (b, t + step)
            )

        def can_send(up, hop):
            return (t - hop + 1 >= 0) & (t + 1 < nt) if up else (t + hop - 1 < nt) & (t >= 1)

        def can_take(up, hop):
            return t - hop >= 0 if up else t + hop < nt

        def send_hop(hop):
            for up in (True, False):
                @pl.when(can_send(up, hop))
                def _():
                    for arr in range(2):
                        along(up, hop, arr, t - hop + 1 if up else t + hop - 1).start()

        def sent_hop(hop):
            for up in (True, False):
                @pl.when(can_send(up, hop))
                def _():
                    for arr in range(2):
                        along(up, hop, arr, t - hop + 1 if up else t + hop - 1).wait_send()

        def take_hop(hop):
            for up in (True, False):
                @pl.when(can_take(up, hop))
                def _():
                    for arr in range(2):
                        shard = t - hop if up else t + hop
                        remote(
                            (W1, W2)[arr].at[shard, mine], (W1, W2)[arr].at[shard, mine],
                            zs.at[int(up), hop, arr], zr.at[int(up), hop, arr], (b, t - 1 if up else t + 1),
                        ).wait_recv()

        for k in range(1, nt):
            bias_copy(k).start()
        send_hop(1)

        def shard_at(k):
            if k == 0:
                return t
            return sum(jnp.where(t == s, near[s][k - 1], 0) for s in range(nt))

        order = [shard_at(k) for k in range(nt)]
        moves = (
            (l, p_first), (l, p_second), (p_first, p_second),
            (l, p_core), (p_first, p_core), (p_second, p_core), (p_both, p_core),
        )

        def plane(k, move):
            who, peer = moves[move]
            part = pl.ds(pl.multiple_of(who * piece, piece), piece)
            return [
                remote(
                    w.at[order[k], part], w.at[order[k], part], ps.at[k, move, arr], pr.at[k, move, arr],
                    (base + peer, t),
                )
                for arr, w in enumerate((W1, W2))
            ]

        def act(k, stage):
            if stage == 0:
                take_hop(k)
                if k + 1 < nt:
                    send_hop(k + 1)
                go = (0, 1)
            elif stage == 1:
                for cp in plane(k, 0):
                    cp.wait_recv()
                go = (2, 3, 4)
            elif stage == 2:
                for move in (1, 2):
                    for cp in plane(k, move):
                        cp.wait_recv()
                go = (5, 6)
            else:
                for move in range(3, 7):
                    for cp in plane(k, move):
                        cp.wait_recv()
                for move in range(7):
                    for cp in plane(k, move):
                        cp.wait_send()
                sent_hop(k)
                if k == 1:
                    for step in range(1, nt):
                        bias_copy(step).wait()
                go = ()
            for move in go:
                for cp in plane(k, move):
                    cp.start()

        plan = {
            (0, 1, 0): [(1, 0)],
            (1, 0, 1): [(1, 1), (2, 0)],
            (1, 1, 1): [(1, 2)],
            (2, 0, 0): [(2, 1), (3, 0)],
            (2, 1, 1): [(2, 2)],
            (2, 1, 2): [(3, 1)],
            (3, 1, 0): [(3, 2)],
        }

        def tick(g, section, step):
            for (gg, ss, when), what in plan.items():
                if (gg, ss) == (g, section):
                    if isinstance(step, int):
                        if step == when:
                            for k, stage in what:
                                act(k, stage)
                        continue

                    @pl.when(step == when)
                    def _():
                        for k, stage in what:
                            act(k, stage)

        def token_forward(g, p, n2x, gpx):
            q = g * pairs + p
            slot = q % SLOTS
            ahead = q + SLOTS - 1

            @pl.when(ahead < nt * pairs)
            def _():
                for cp in fetch(ahead, ahead % SLOTS):
                    cp.start()

            for cp in fetch(q, slot):
                cp.wait()

            grp = (t + 1 + g) % nt
            both_x = xb[slot]
            both_g = jnp.swapaxes(gb[slot], 0, 1)
            for e in range(2):
                i = 2 * p + e
                at = pl.multiple_of(i * SP, 16)
                x = both_x[:, e, :].astype(F32)
                scaled, _ = normal(x)
                n1 = (scaled * g1_r[...] + b1_r[...]).astype(BF)
                th = dot(w1t[...], n1) + tb1c[...]
                r, _ = gelu_parts(th)
                ta = (th * r).astype(BF)
                u = x + dot(w2t[...], ta) + tb2c[...]
                if g == nt - 1:
                    n1_s[i, 0:S, :] = n1
                    ta_s[i] = ta
                    u_s[i] = u
                scaled, _ = normal(u)
                n2x[pl.ds(at, S), :] = (scaled * g2_r[...] + b2_r[...]).astype(BF)
                valid = jnp.where(own * grp + i < cnt[0], 0.5, 0.0)
                gpx[pl.ds(at, S), :] = both_g[e] * jnp.full((1, D), valid, F32).astype(BF)

        def hidden(rr, n2x, gpx, w1, w2, bias, slot):
            ch = dot(n2x[rr, :], w1) + bias
            da = dot_nt(gpx[rr, :], w2)
            r, s = gelu_parts(ch)
            ca[slot, rr, :] = (ch * r).astype(BF)
            grad = da * slope_twice(r, s)
            return grad, grad.astype(BF)

        def chunk_at(j):
            return pl.ds(pl.multiple_of(j * chunk, 16), chunk)

        def first(p, carry):
            token_forward(0, p, n2a, gpa)
            return carry

        lax.fori_loop(0, pairs, first, 0)
        for cp in local:
            cp.wait()
        dacc[...] = jnp.zeros_like(dacc)

        for g in range(nt):
            n2x, gpx = ((n2a, gpa), (n2b, gpb))[g % 2]
            n2y, gpy = ((n2b, gpb), (n2a, gpa))[g % 2]

            def step(j, carry):
                tick(g, 0, j)
                rr = chunk_at(j)
                grad, dh = hidden(rr, n2x, gpx, W1[t], W2[t], B1[t], 0)
                dch[rr, :] = dh
                gcb1[...] += total_of(grad)
                return carry

            lax.fori_loop(0, n_chunk, step, 0)

            def weights(p, carry):
                tick(g, 1, p)
                if g + 1 < nt:
                    token_forward(g + 1, p, n2y, gpy)
                ks = pl.ds(pl.multiple_of(p * third, third), third)
                acc[1, ks, :] += dot_tn(ca[0, :, ks], gpx[...])
                acc[0, ks, :] += dot_tn(n2x[:, ks], dch[...])
                return carry

            if g + 1 < nt:
                lax.fori_loop(0, pairs, weights, 0)
            else:
                for p in range(pairs):
                    tick(g, 1, p)
                acc[1] += dot_tn(ca[0], gpx[...])
                acc[0] += dot_tn(n2x[...], dch[...])
        n2, gp = ((n2a, gpa), (n2b, gpb))[(nt - 1) % 2]

        half, quarter = D // 2, D // 4
        bit_f = (1 - c) * ((l // 2) % 2) + c * ((l // 4) % 2)
        bit_s = (1 - c) * ((l // 4) % 2) + c * ((l // 2) % 2)

        def span(start, size):
            return pl.ds(pl.multiple_of(start, quarter), size)

        here_f = span(bit_f * half, half)
        there_f = span((1 - bit_f) * half, half)
        here_s = span(bit_f * half + bit_s * quarter, quarter)
        there_s = span(bit_f * half + (1 - bit_s) * quarter, quarter)

        idle_n, idle_g = ((n2b, gpb), (n2a, gpa))[(nt - 1) % 2]
        sends = (idle_n.at[0:D], idle_g.at[0:half], idle_g.at[half : half + quarter])

        def sum_copy(stage):
            if stage < 3:
                src = sends[stage]
                dst = (rcv0, rcv1, rcv2)[stage]
                peer = (p_core, p_first, p_second)[stage]
            else:
                src = (gwb.at[c, here_s], gwb.at[c, here_f], gwb.at[c])[stage - 3]
                dst = src
                peer = (p_second, p_first, p_core)[stage - 3]
            return remote(src, dst, as_.at[stage], ar_.at[stage], (base + peer, t))

        def sum_step(stage):
            if stage > 0:
                sum_copy(stage - 1).wait()
            if stage == 0:
                sends[0][...] = acc[1 - c].astype(BF)
                sum_copy(0).start()
            elif stage == 1:
                sends[1][...] = (acc[c, there_f, :] + rcv0[there_f, :].astype(F32)).astype(BF)
                sum_copy(1).start()
                acc[c, here_f, :] += rcv0[here_f, :].astype(F32)
            elif stage == 2:
                sends[2][...] = (
                    acc[c, there_s, :] + rcv1[span((1 - bit_s) * quarter, quarter), :].astype(F32)
                ).astype(BF)
                sum_copy(2).start()
                acc[c, here_s, :] += rcv1[span(bit_s * quarter, quarter), :].astype(F32)
            elif stage == 3:
                total = acc[c, here_s, :] + rcv2[...].astype(F32)
                for n, e in enumerate(extra):
                    spare = idle_g.at[span(half + (n + 1) * quarter, quarter)]
                    spare[...] = total.astype(BF)
                    cp = remote(spare, rcvx.at[n], axs.at[n], axr.at[n], (flip(b, e), t))
                    cp.start()
                    cp.wait()
                    total = spare[...].astype(F32) + rcvx[n].astype(F32)
                gwb[c, here_s, :] = total.astype(BF)
                sum_copy(3).start()
            elif stage < 6:
                sum_copy(stage).start()

        sum_step(0)

        late = {2: 1, 7: 2}

        def gather(j, grad):
            for e in range(2):
                dacc[2 * j + e] += grad[e * SP : e * SP + S, :]

        def back(rr, k):
            return dot_nt(dch[rr, :], W1[order[k]])

        for k in range(1, nt - 1):
            def other(j, carry):
                if k == 1:
                    @pl.when(j == 0)
                    def _():
                        act(1, 3)
                else:
                    @pl.when(j == 0)
                    def _():
                        act(2, 3)
                for when, stage in late.items():
                    if when // n_chunk == k - 1:
                        @pl.when(j == when % n_chunk)
                        def _():
                            sum_step(stage)
                rr = chunk_at(j)
                gather(j, back(rr, k - 1))
                shard = order[k]
                dch[rr, :] = hidden(rr, n2, gp, W1[shard], W2[shard], B1[shard], k)[1]
                return carry

            lax.fori_loop(0, n_chunk, other, 0)

        def last(j):
            rr = chunk_at(j)
            k = nt - 1
            earlier = back(rr, k - 1)
            shard = order[k]
            dh = hidden(rr, n2, gp, W1[shard], W2[shard], B1[shard], k)[1]
            gather(j, earlier + dot_nt(dh, W1[shard]))

        def xcopy(p, slot):
            at = pl.ds(own * t + 2 * p, 2)
            return pltpu.make_async_copy(img.at[:, at, :], xb.at[slot], x_sem.at[slot])

        def gcopy(i):
            return pltpu.make_async_copy(dacc.at[i], gim_h.at[i], i_sem.at[i])

        def token_back(p):
            slot = p
            xcopy(p, slot).wait()
            both_x = xb[slot]
            both = [dacc[2 * p + e] for e in range(2)]
            for e in range(2):
                i = 2 * p + e
                at = pl.multiple_of(i * SP, 16)
                dn2 = both[e]
                g = gp[pl.ds(at, S), :].astype(F32) * 2.0
                scaled, inverse = normal(u_s[i])
                vec[0:1, :] += total_of(dn2 * scaled)
                vec[1:2, :] += total_of(dn2)
                vec[4:5, :] += total_of(g)
                du = g + norm_back(dn2, g2_r[...], scaled, inverse)
                dz = du.astype(BF)
                tb2acc[...] += jnp.sum(dz.astype(F32), axis=1, keepdims=True)
                n1 = n1_s[i]
                sm_r[SP : SP + S, :] += dot_nt(dz, ta_s[i])
                th = dot(w1t[...], n1[0:S, :]) + tb1c[...]
                r, s = gelu_parts(th)
                dth = (dot(tw2_r[...], dz) * slope_twice(r, s)).astype(BF)
                sm_r[0:SP, :] += dot_nt(n1, dth)
                dn1 = dot(tw1_r[...], dth)
                scaled, inverse = normal(both_x[:, e, :].astype(F32))
                vec[2:3, :] += total_of(dn1 * scaled)
                vec[3:4, :] += total_of(dn1)
                dacc[i] = du + norm_back(dn1, g1_r[...], scaled, inverse)

        def flush_pair(p):
            for e in range(2):
                gcopy(2 * p + e).start()

        def ocopy(i):
            return pltpu.make_async_copy(outs.at[i], out_h.at[i], o_sem.at[i])

        def flush_result(j):
            for e in range(2):
                ocopy(2 * j + e).start()

        def result(j):
            rr = chunk_at(j)
            total = dot(ca[0, rr, :], W2[t])
            for k in range(1, nt):
                total += dot(ca[k, rr, :], W2[order[k]])
            for e in range(2):
                v = total[e * SP : e * SP + S, :] * 0.5 + u_s[2 * j + e] + cb2_r[...]
                outs[2 * j + e] = v.astype(BF)

        for p in range(pairs):
            xcopy(p, p).start()
        act(3, 3)

        def final(j, carry):
            @pl.when(j == 1)
            def _():
                sum_step(2)

            last(j)
            return carry

        lax.fori_loop(0, n_chunk, final, 0)

        def token(p, carry):
            @pl.when(p == 1)
            def _():
                sum_step(3)


            token_back(p)
            flush_pair(p)
            return carry

        lax.fori_loop(0, pairs, token, 0)

        low = 2 * SP
        sm_r[SP : SP + S, :] = sm_r[SP : SP + S, :] * 0.5
        for k in range(5):
            for h in range(2):
                sm_r[low + 2 * k + h : low + 2 * k + h + 1, :] = vec[k : k + 1, h * HD : (h + 1) * HD]
        sm_r[low + 10 : low + 11, 0:S] = total_of(eye(S, F32) * tb2acc[...])
        for s in range(nt):
            for h in range(2):
                r = low + 11 + 2 * s + h
                sm_r[r : r + 1, :] = jnp.where(t == s, 1.0, 0.0) * gcb1[:, h * HD : (h + 1) * HD]

        part = SMALL // RING
        s_snd[...] = sm_r[...].astype(BF)

        def eighths(k, back):
            whom = (base + (l + k) % RING, t)
            if back:
                ref = s_all.at[pl.ds(pl.multiple_of(l * part, part), part)]
                return remote(ref, ref, sqs.at[k], sqr.at[k], whom)
            src = s_snd.at[pl.ds(pl.multiple_of(((l + k) % RING) * part, part), part)]
            return remote(src, s_rcv.at[k], sps.at[k], spr.at[k], whom)

        def across(k):
            return remote(z_rcv.at[t], z_rcv.at[t], szs.at[k], szr.at[k], (b, (t + k) % nt))

        for k in range(1, RING):
            eighths(k, False).start()

        def small_step(stage):
            if stage == 1:
                total = sm_r[pl.ds(pl.multiple_of(l * part, part), part), :]
                for k in range(1, RING):
                    eighths(k, False).wait()
                    total += s_rcv[k].astype(F32)
                z_rcv[t] = total.astype(BF)
                for k in range(1, nt):
                    across(k).start()
            elif stage == 2:
                for k in range(1, nt):
                    across(k).wait()
                total = z_rcv[0].astype(F32)
                for s in range(1, nt):
                    total += z_rcv[s].astype(F32)
                for n, e in enumerate(extra):
                    x_snd[n] = total.astype(BF)
                    cp = remote(x_snd.at[n], x_rcv.at[n], sxs.at[n], sxr.at[n], (flip(b, e), t))
                    cp.start()
                    cp.wait()
                    total = x_snd[n].astype(F32) + x_rcv[n].astype(F32)
                s_all[pl.ds(pl.multiple_of(l * part, part), part), :] = total.astype(BF)
                for k in range(1, RING):
                    eighths(k, True).start()
            else:
                for k in range(1, RING):
                    eighths(k, True).wait()

        def rest(j, carry):
            @pl.when(j == 0)
            def _():
                sum_step(4)

            result(j)
            flush_result(j)
            return carry

        lax.fori_loop(0, n_chunk, rest, 0)
        small_step(1)
        sum_step(5)
        small_step(2)
        sum_copy(5).wait()
        flush = pltpu.make_async_copy(gwb, gwb_o, l_sem.at[0])
        flush.start()
        for i in range(own):
            ocopy(i).wait()
            gcopy(i).wait()
        small_step(3)
        flush.wait()

    V = pltpu.VMEM
    DMA = pltpu.SemaphoreType.DMA
    any_ = pl.BlockSpec(memory_space=pl.ANY)
    vm = pl.BlockSpec(memory_space=V)
    f = lambda *shape: jax.ShapeDtypeStruct(shape, F32)
    h = lambda *shape: jax.ShapeDtypeStruct(shape, BF)
    xn = max(1, len(extra))
    part = SMALL // RING
    raw = pl.pallas_call(
        kernel,
        out_shape=(h(own, S, D), f(own, S, D), h(2, D, D), h(SMALL, DS)),
        in_specs=[any_, any_, any_, any_, vm, pl.BlockSpec(memory_space=pltpu.SMEM)] + [vm] * 9,
        out_specs=(any_, any_, any_, vm),
        scratch_shapes=[
            V((nt, D, H), BF), V((nt, H, D), BF), V((nt, 1, H), F32),
            V((SLOTS, S, 2, D), BF), V((SLOTS, S, 2, D), BF),
            V((rows, D), BF), V((rows, D), BF), V((rows, D), BF), V((rows, D), BF),
            V((nt, rows, H), BF), V((rows, H), BF), V((own, S, D), F32),
            V((own, S, D), F32), V((own, DS, D), BF), V((own, SP, D), BF),
            V((DS, S), BF), V((S, DS), BF), V((DS, S), BF), V((DS, 1), F32), V((S, 1), F32),
            V((1, H), F32), V((8, D), F32), V((S, 1), F32), V((own, S, D), BF),
            V((1, H), F32), V((1, D), F32), V((1, D), F32), V((1, D), F32), V((1, D), F32), V((1, D), F32),
            V((2, D, D), F32), V((SMALL, DS), F32),
            V((D, D), BF), V((D // 2, D), BF), V((D // 4, D), BF),
            V((xn, D // 4, D), BF), V((2, D, D), BF),
            V((SMALL, DS), BF), V((RING, part, DS), BF), V((nt, part, DS), BF),
            V((xn, part, DS), BF), V((xn, part, DS), BF),
            DMA((SLOTS,)), DMA((SLOTS,)), DMA((2,)), DMA((own,)), DMA((own,)),
            DMA((2, nt, 2)), DMA((2, nt, 2)), DMA((nt, 7, 2)), DMA((nt, 7, 2)), DMA((nt,)), DMA((nt,)),
            DMA((6,)), DMA((6,)), DMA((xn,)), DMA((xn,)), DMA((RING,)), DMA((RING,)), DMA((nt,)), DMA((nt,)),
            DMA((xn,)), DMA((xn,)), DMA((RING,)), DMA((RING,)),
        ],
        compiler_params=pltpu.CompilerParams(
            collective_id=0, has_side_effects=True, vmem_limit_bytes=65200 * 1024
        ),
    )(
        jnp.swapaxes(images, 0, 1), jnp.swapaxes(cot, 0, 1), cw1, cw2, cb1, counts,
        g1, b1, g2, b2, tw1, tw2.T, tb1, tb2, cb2,
    )

    def unpack(
        out_r, gim_r, gwb_r, s_all,
        out_o, gim_o, gg1_o, gb1_o, gtw1_o, gtb1_o, gtw2_o, gtb2_o, gg2_o, gb2_o, gw1_o, gcb1_o, gw2_o, gcb2_o,
        o_s, m_s, b_s, w_s, sem_in, sem,
    ):
        t = lax.axis_index("tensor")
        cuts = [(gwb_r.at[n], b_s.at[n]) for n in range(2)]
        cuts += [(gim_r.at[i], m_s.at[i]) for i in range(own)]
        cuts += [(out_r.at[i], o_s.at[i]) for i in range(own)]
        goals = [gw1_o, gw2_o] + [gim_o.at[i] for i in range(own)] + [out_o.at[i] for i in range(own)]
        loads = [pltpu.make_async_copy(src, dst, sem_in.at[n]) for n, (src, dst) in enumerate(cuts)]
        for cp in loads:
            cp.start()
        moves = []
        for n, ref in enumerate(goals):
            loads[n].wait()
            src = cuts[n][1]
            if n < 2:
                w_s[n] = b_s[n].astype(F32)
                src = w_s.at[n]
            moves.append(pltpu.make_async_copy(src, ref, sem.at[n]))
            moves[-1].start()
        low = 2 * SP
        gtw1_o[...] = s_all[0:S, :].astype(F32)
        gtw2_o[...] = s_all[SP : SP + S, :].astype(F32)
        ends = s_all[low : low + 32, :].astype(F32)
        at = S // 16 * 16
        gtb1_o[...] = s_all[at : at + 16, :].astype(F32)[S - at]
        gtb2_o[...] = ends[10, 0:S]
        for k, ref in enumerate((gg2_o, gb2_o, gg1_o, gb1_o, gcb2_o)):
            for h in range(2):
                ref[h * HD : (h + 1) * HD] = ends[2 * k + h]
        for h in range(2):
            total = ends[11 + h] * jnp.where(t == 0, 1.0, 0.0)
            for s in range(1, nt):
                total += ends[11 + 2 * s + h] * jnp.where(t == s, 1.0, 0.0)
            gcb1_o[h * HD : (h + 1) * HD] = total
        for cp in moves:
            cp.wait()

    out = pl.pallas_call(
        unpack,
        out_shape=(
            h(own, S, D), f(own, S, D), f(D), f(D), f(S, DS), f(DS), f(S, DS), f(S), f(D), f(D),
            f(D, H), f(H), f(H, D), f(D),
        ),
        in_specs=[any_, any_, any_, vm],
        out_specs=(any_, any_) + (vm,) * 8 + (any_, vm, any_, vm),
        scratch_shapes=[
            V((own, S, D), BF), V((own, S, D), F32), V((2, D, D), BF), V((2, D, D), F32),
            DMA((2 + 2 * own,)), DMA((2 + 2 * own,)),
        ],
        compiler_params=pltpu.CompilerParams(vmem_limit_bytes=65200 * 1024),
    )(*raw)
    return out[:6] + (out[6].T,) + out[7:]


def solution(mesh):
    nb, nt = mesh.shape["batch"], mesh.shape["tensor"]
    in_specs = (
        P("batch", None, None), P("batch"),
        P(), P(), P(), P(), P(), P(), P(), P(),
        P(None, "tensor"), P("tensor"), P("tensor", None), P(),
        P("batch", None, None),
    )
    both = P(("batch", "tensor"), None, None)
    out_specs = (
        both, both,
        P(), P(), P(), P(), P(), P(), P(), P(),
        P(None, "tensor"), P("tensor"), P("tensor", None), P(),
    )
    return jax.shard_map(
        lambda *args: per_device(nb, nt, args),
        mesh=mesh, in_specs=in_specs, out_specs=out_specs, check_vma=False,
    )
```

```python
import jax
import jax.numpy as jnp
from jax import lax
from jax.experimental import pallas as pl
from jax.experimental.pallas import tpu as pltpu
from jax.sharding import PartitionSpec as P

EPSILON = 1e-06
ROOT_HALF = 0.7071067811865476
INV_ROOT_TAU = 0.3989422804014327
LOG2_E = 1.4426950408889634
MESH = pl.DeviceIdType.MESH
BF = jnp.bfloat16
F32 = jnp.float32
SLOTS = 3
RING = 8
SMALL = 512


def dot(a, b):
    return lax.dot_general(a, b, (((1,), (0,)), ((), ())), preferred_element_type=F32)


def dot_nt(a, b):
    return lax.dot_general(a, b, (((1,), (1,)), ((), ())), preferred_element_type=F32)


def dot_tn(a, b):
    return lax.dot_general(a, b, (((0,), (0,)), ((), ())), preferred_element_type=F32)


def flip(v, bit):
    step = 1 << bit
    return v + (1 - 2 * ((v // step) % 2)) * step


def normal(v):
    center = v - jnp.mean(v, axis=-1, keepdims=True)
    inverse = lax.rsqrt(jnp.mean(center * center, axis=-1, keepdims=True) + EPSILON)
    return center * inverse, inverse


def gelu_parts(v):
    s = v * ROOT_HALF
    return 1.0 + lax.erf(s), s


def slope_twice(r, s):
    return r + (s * jnp.exp2(s * s * -LOG2_E)) * (2.0 * INV_ROOT_TAU / ROOT_HALF)


def norm_back(grad, gain, scaled, inverse):
    weighted = grad * gain
    return inverse * (
        weighted
        - jnp.mean(weighted, axis=-1, keepdims=True)
        - scaled * jnp.mean(weighted * scaled, axis=-1, keepdims=True)
    )


def eye(n, dtype, value=1.0):
    rows = lax.broadcasted_iota(jnp.int32, (n, n), 0)
    cols = lax.broadcasted_iota(jnp.int32, (n, n), 1)
    return jnp.where(rows == cols, value, 0.0).astype(dtype)


def column(row):
    n = row.shape[1]
    return jnp.sum(eye(n, F32) * row, axis=1, keepdims=True)


def total_of(v):
    return jnp.sum(v, axis=0, keepdims=True)


def per_device(nb, nt, args):
    (images, counts, g1, b1, tw1, tb1, tw2, tb2, g2, b2, cw1, cb1, cw2, cb2, cot) = args
    slots, S, D = images.shape
    DS = tw1.shape[1]
    H = cw1.shape[1]
    own = slots // nt
    SP = -(-S // 16) * 16
    pairs = own // 2
    rows = own * SP
    chunk = 2 * SP
    n_chunk = rows // chunk
    third = D // pairs
    piece = D // RING
    HD = D // 2
    near = [sorted((s for s in range(nt) if s != t), key=lambda s: (abs(s - t), s)) for t in range(nt)]
    if nt == 4:
        near[2] = [3, 1, 0]
    extra = range(3, nb.bit_length() - 1)

    def kernel(
        img, cot_h, w1_h, w2_h, cb1_1, cnt, g1_1, b1_1, g2_1, b2_1, tw1_r, w2t_r, tb1_1, tb2_1, cb2_1,
        out_h, gim_h, gwb_o, s_all,
        W1, W2, B1, xb, gb, n2a, n2b, gpa, gpb, ca, dch, dacc, u_s, ta_s, n1_s, w1t, w2t, tw2_r, tb1c, tb2c,
        gcb1, vec, tb2acc, outs,
        cb1_r, g1_r, b1_r, g2_r, b2_r, cb2_r, acc, sm_r, rcv0, rcv1, rcv2, rcvx, gwb,
        s_snd, s_rcv, z_rcv, x_snd, x_rcv,
        x_sem, g_sem, l_sem, o_sem, i_sem, zs, zr, ps, pr, bs, br,
        as_, ar_, axs, axr, sps, spr, szs, szr, sxs, sxr, sqs, sqr,
    ):
        b = lax.axis_index("batch")
        t = lax.axis_index("tensor")
        l = b % RING
        base = b - l
        c = l % 2
        lf, ls = flip(l, 1), flip(l, 2)
        p_first = (1 - c) * lf + c * ls
        p_second = (1 - c) * ls + c * lf
        p_both = flip(flip(l, 1), 2)
        p_core = flip(l, 0)

        def remote(src, dst, ss, rs, dev):
            return pltpu.make_async_remote_copy(src, dst, ss, rs, device_id=dev, device_id_type=MESH)

        bar = pltpu.get_barrier_semaphore()
        partners = [(b, (t + k) % nt) for k in range(1, nt)]
        partners += [(base + (l + k) % RING, t) for k in range(1, RING)]
        partners += [(flip(b, e), t) for e in extra]
        for d in partners:
            pl.semaphore_signal(bar, inc=1, device_id=d, device_id_type=MESH)

        def fetch(q, slot):
            grp = (t + 1 + q // pairs) % nt
            at = pl.ds(own * grp + 2 * (q % pairs), 2)
            return (
                pltpu.make_async_copy(img.at[:, at, :], xb.at[slot], x_sem.at[slot]),
                pltpu.make_async_copy(cot_h.at[:, at, :], gb.at[slot], g_sem.at[slot]),
            )

        for q in range(SLOTS - 1):
            for cp in fetch(q, q):
                cp.start()
        local = [
            pltpu.make_async_copy(w1_h, W1.at[t], l_sem.at[0]),
            pltpu.make_async_copy(w2_h, W2.at[t], l_sem.at[1]),
        ]
        for cp in local:
            cp.start()

        cb1_r[...] = cb1_1[...].reshape(1, H)
        for ref, one in ((g1_r, g1_1), (b1_r, b1_1), (g2_r, g2_1), (b2_r, b2_1), (cb2_r, cb2_1)):
            ref[...] = one[...].reshape(1, D)
        B1[t] = cb1_r[...]
        w1t[...] = dot_nt(eye(DS, BF), tw1_r[...]).astype(BF)
        w2t[...] = (w2t_r[...].astype(F32) * 0.5).astype(BF)
        tw2_r[...] = dot_nt(eye(DS, BF), w2t[...]).astype(BF)
        tb1c[...] = column(tb1_1[...].reshape(1, DS))
        tb2c[...] = column(tb2_1[...].reshape(1, S))
        acc[...] = jnp.zeros_like(acc)
        gcb1[...] = jnp.zeros_like(gcb1)
        vec[...] = jnp.zeros_like(vec)
        tb2acc[...] = jnp.zeros_like(tb2acc)
        sm_r[...] = jnp.zeros_like(sm_r)
        pad = SP - S
        for i in range(own):
            for ref in (n2a, n2b, gpa, gpb):
                ref[i * SP + S : (i + 1) * SP, :] = jnp.zeros((pad, D), BF)
            n1_s[i, S:SP, :] = jnp.where(
                lax.broadcasted_iota(jnp.int32, (pad, D), 0) == 0, 1.0, 0.0
            ).astype(BF)

        pl.semaphore_wait(bar, len(partners))

        mine = pl.ds(pl.multiple_of(l * piece, piece), piece)

        def bias_copy(k):
            return remote(cb1_r, B1.at[t], bs.at[k], br.at[k], (b, (t + k) % nt))

        def along(up, hop, arr, shard):
            src = (w1_h, w2_h)[arr].at[mine] if hop == 1 else (W1, W2)[arr].at[shard, mine]
            step = 1 if up else -1
            return remote(
                src, (W1, W2)[arr].at[shard, mine], zs.at[int(up), hop, arr], zr.at[int(up), hop, arr], (b, t + step)
            )

        def can_send(up, hop):
            return (t - hop + 1 >= 0) & (t + 1 < nt) if up else (t + hop - 1 < nt) & (t >= 1)

        def can_take(up, hop):
            return t - hop >= 0 if up else t + hop < nt

        def send_hop(hop):
            for up in (True, False):
                @pl.when(can_send(up, hop))
                def _():
                    for arr in range(2):
                        along(up, hop, arr, t - hop + 1 if up else t + hop - 1).start()

        def sent_hop(hop):
            for up in (True, False):
                @pl.when(can_send(up, hop))
                def _():
                    for arr in range(2):
                        along(up, hop, arr, t - hop + 1 if up else t + hop - 1).wait_send()

        def take_hop(hop):
            for up in (True, False):
                @pl.when(can_take(up, hop))
                def _():
                    for arr in range(2):
                        shard = t - hop if up else t + hop
                        remote(
                            (W1, W2)[arr].at[shard, mine], (W1, W2)[arr].at[shard, mine],
                            zs.at[int(up), hop, arr], zr.at[int(up), hop, arr], (b, t - 1 if up else t + 1),
                        ).wait_recv()

        for k in range(1, nt):
            bias_copy(k).start()
        send_hop(1)

        def shard_at(k):
            if k == 0:
                return t
            return sum(jnp.where(t == s, near[s][k - 1], 0) for s in range(nt))

        order = [shard_at(k) for k in range(nt)]
        moves = (
            (l, p_first), (l, p_second), (p_first, p_second),
            (l, p_core), (p_first, p_core), (p_second, p_core), (p_both, p_core),
        )

        def plane(k, move):
            who, peer = moves[move]
            part = pl.ds(pl.multiple_of(who * piece, piece), piece)
            return [
                remote(
                    w.at[order[k], part], w.at[order[k], part], ps.at[k, move, arr], pr.at[k, move, arr],
                    (base + peer, t),
                )
                for arr, w in enumerate((W1, W2))
            ]

        def act(k, stage):
            if stage == 0:
                take_hop(k)
                if k + 1 < nt:
                    send_hop(k + 1)
                go = (0, 1)
            elif stage == 1:
                for cp in plane(k, 0):
                    cp.wait_recv()
                go = (2, 3, 4)
            elif stage == 2:
                for move in (1, 2):
                    for cp in plane(k, move):
                        cp.wait_recv()
                go = (5, 6)
            else:
                for move in range(3, 7):
                    for cp in plane(k, move):
                        cp.wait_recv()
                for move in range(7):
                    for cp in plane(k, move):
                        cp.wait_send()
                sent_hop(k)
                if k == 1:
                    for step in range(1, nt):
                        bias_copy(step).wait()
                go = ()
            for move in go:
                for cp in plane(k, move):
                    cp.start()

        plan = {
            (0, 1, 0): [(1, 0)],
            (1, 0, 1): [(1, 1), (2, 0)],
            (1, 1, 1): [(1, 2)],
            (2, 0, 0): [(2, 1), (3, 0)],
            (2, 1, 1): [(2, 2)],
            (2, 1, 2): [(3, 1)],
            (3, 1, 0): [(3, 2)],
        }

        def tick(g, section, step):
            for (gg, ss, when), what in plan.items():
                if (gg, ss) == (g, section):
                    if isinstance(step, int):
                        if step == when:
                            for k, stage in what:
                                act(k, stage)
                        continue

                    @pl.when(step == when)
                    def _():
                        for k, stage in what:
                            act(k, stage)

        def token_forward(g, p, n2x, gpx):
            q = g * pairs + p
            slot = q % SLOTS
            ahead = q + SLOTS - 1

            @pl.when(ahead < nt * pairs)
            def _():
                for cp in fetch(ahead, ahead % SLOTS):
                    cp.start()

            for cp in fetch(q, slot):
                cp.wait()

            grp = (t + 1 + g) % nt
            both_x = xb[slot]
            both_g = jnp.swapaxes(gb[slot], 0, 1)
            for e in range(2):
                i = 2 * p + e
                at = pl.multiple_of(i * SP, 16)
                x = both_x[:, e, :].astype(F32)
                scaled, _ = normal(x)
                n1 = (scaled * g1_r[...] + b1_r[...]).astype(BF)
                th = dot(w1t[...], n1) + tb1c[...]
                r, _ = gelu_parts(th)
                ta = (th * r).astype(BF)
                u = x + dot(w2t[...], ta) + tb2c[...]
                if g == nt - 1:
                    n1_s[i, 0:S, :] = n1
                    ta_s[i] = ta
                    u_s[i] = u
                scaled, _ = normal(u)
                n2x[pl.ds(at, S), :] = (scaled * g2_r[...] + b2_r[...]).astype(BF)
                valid = jnp.where(own * grp + i < cnt[0], 0.5, 0.0)
                gpx[pl.ds(at, S), :] = both_g[e] * jnp.full((1, D), valid, F32).astype(BF)

        def hidden(rr, n2x, gpx, w1, w2, bias, slot):
            ch = dot(n2x[rr, :], w1) + bias
            da = dot_nt(gpx[rr, :], w2)
            r, s = gelu_parts(ch)
            ca[slot, rr, :] = (ch * r).astype(BF)
            grad = da * slope_twice(r, s)
            return grad, grad.astype(BF)

        def chunk_at(j):
            return pl.ds(pl.multiple_of(j * chunk, 16), chunk)

        def first(p, carry):
            token_forward(0, p, n2a, gpa)
            return carry

        lax.fori_loop(0, pairs, first, 0)
        for cp in local:
            cp.wait()
        dacc[...] = jnp.zeros_like(dacc)

        for g in range(nt):
            n2x, gpx = ((n2a, gpa), (n2b, gpb))[g % 2]
            n2y, gpy = ((n2b, gpb), (n2a, gpa))[g % 2]

            def step(j, carry):
                tick(g, 0, j)
                rr = chunk_at(j)
                grad, dh = hidden(rr, n2x, gpx, W1[t], W2[t], B1[t], 0)
                dch[rr, :] = dh
                gcb1[...] += total_of(grad)
                return carry

            lax.fori_loop(0, n_chunk, step, 0)

            def weights(p, carry):
                tick(g, 1, p)
                if g + 1 < nt:
                    token_forward(g + 1, p, n2y, gpy)
                ks = pl.ds(pl.multiple_of(p * third, third), third)
                acc[1, ks, :] += dot_tn(ca[0, :, ks], gpx[...])
                acc[0, ks, :] += dot_tn(n2x[:, ks], dch[...])
                return carry

            if g + 1 < nt:
                lax.fori_loop(0, pairs, weights, 0)
            else:
                for p in range(pairs):
                    tick(g, 1, p)
                acc[1] += dot_tn(ca[0], gpx[...])
                acc[0] += dot_tn(n2x[...], dch[...])
        n2, gp = ((n2a, gpa), (n2b, gpb))[(nt - 1) % 2]

        half, quarter = D // 2, D // 4
        bit_f = (1 - c) * ((l // 2) % 2) + c * ((l // 4) % 2)
        bit_s = (1 - c) * ((l // 4) % 2) + c * ((l // 2) % 2)

        def span(start, size):
            return pl.ds(pl.multiple_of(start, quarter), size)

        here_f = span(bit_f * half, half)
        there_f = span((1 - bit_f) * half, half)
        here_s = span(bit_f * half + bit_s * quarter, quarter)
        there_s = span(bit_f * half + (1 - bit_s) * quarter, quarter)

        idle_n, idle_g = ((n2b, gpb), (n2a, gpa))[(nt - 1) % 2]
        sends = (idle_n.at[0:D], idle_g.at[0:half], idle_g.at[half : half + quarter])

        def sum_copy(stage):
            if stage < 3:
                src = sends[stage]
                dst = (rcv0, rcv1, rcv2)[stage]
                peer = (p_core, p_first, p_second)[stage]
            else:
                src = (gwb.at[c, here_s], gwb.at[c, here_f], gwb.at[c])[stage - 3]
                dst = src
                peer = (p_second, p_first, p_core)[stage - 3]
            return remote(src, dst, as_.at[stage], ar_.at[stage], (base + peer, t))

        def sum_step(stage):
            if stage > 0:
                sum_copy(stage - 1).wait()
            if stage == 0:
                sends[0][...] = acc[1 - c].astype(BF)
                sum_copy(0).start()
            elif stage == 1:
                sends[1][...] = (acc[c, there_f, :] + rcv0[there_f, :].astype(F32)).astype(BF)
                sum_copy(1).start()
                acc[c, here_f, :] += rcv0[here_f, :].astype(F32)
            elif stage == 2:
                sends[2][...] = (
                    acc[c, there_s, :] + rcv1[span((1 - bit_s) * quarter, quarter), :].astype(F32)
                ).astype(BF)
                sum_copy(2).start()
                acc[c, here_s, :] += rcv1[span(bit_s * quarter, quarter), :].astype(F32)
            elif stage == 3:
                total = acc[c, here_s, :] + rcv2[...].astype(F32)
                for n, e in enumerate(extra):
                    spare = idle_g.at[span(half + (n + 1) * quarter, quarter)]
                    spare[...] = total.astype(BF)
                    cp = remote(spare, rcvx.at[n], axs.at[n], axr.at[n], (flip(b, e), t))
                    cp.start()
                    cp.wait()
                    total = spare[...].astype(F32) + rcvx[n].astype(F32)
                gwb[c, here_s, :] = total.astype(BF)
                sum_copy(3).start()
            elif stage < 6:
                sum_copy(stage).start()

        sum_step(0)

        late = {2: 1, 7: 2}

        def gather(j, grad):
            for e in range(2):
                dacc[2 * j + e] += grad[e * SP : e * SP + S, :]

        def back(rr, k):
            return dot_nt(dch[rr, :], W1[order[k]])

        for k in range(1, nt - 1):
            def other(j, carry):
                if k == 1:
                    @pl.when(j == 0)
                    def _():
                        act(1, 3)
                else:
                    @pl.when(j == 0)
                    def _():
                        act(2, 3)
                for when, stage in late.items():
                    if when // n_chunk == k - 1:
                        @pl.when(j == when % n_chunk)
                        def _():
                            sum_step(stage)
                rr = chunk_at(j)
                gather(j, back(rr, k - 1))
                shard = order[k]
                dch[rr, :] = hidden(rr, n2, gp, W1[shard], W2[shard], B1[shard], k)[1]
                return carry

            lax.fori_loop(0, n_chunk, other, 0)

        def last(j):
            rr = chunk_at(j)
            k = nt - 1
            earlier = back(rr, k - 1)
            shard = order[k]
            dh = hidden(rr, n2, gp, W1[shard], W2[shard], B1[shard], k)[1]
            gather(j, earlier + dot_nt(dh, W1[shard]))

        def xcopy(p, slot):
            at = pl.ds(own * t + 2 * p, 2)
            return pltpu.make_async_copy(img.at[:, at, :], xb.at[slot], x_sem.at[slot])

        def gcopy(i):
            return pltpu.make_async_copy(dacc.at[i], gim_h.at[i], i_sem.at[i])

        def token_back(p):
            slot = p
            xcopy(p, slot).wait()
            both_x = xb[slot]
            both = [dacc[2 * p + e] for e in range(2)]
            for e in range(2):
                i = 2 * p + e
                at = pl.multiple_of(i * SP, 16)
                dn2 = both[e]
                g = gp[pl.ds(at, S), :].astype(F32) * 2.0
                scaled, inverse = normal(u_s[i])
                vec[0:1, :] += total_of(dn2 * scaled)
                vec[1:2, :] += total_of(dn2)
                vec[4:5, :] += total_of(g)
                du = g + norm_back(dn2, g2_r[...], scaled, inverse)
                dz = du.astype(BF)
                tb2acc[...] += jnp.sum(dz.astype(F32), axis=1, keepdims=True)
                n1 = n1_s[i]
                sm_r[SP : SP + S, :] += dot_nt(dz, ta_s[i])
                th = dot(w1t[...], n1[0:S, :]) + tb1c[...]
                r, s = gelu_parts(th)
                dth = (dot(tw2_r[...], dz) * slope_twice(r, s)).astype(BF)
                sm_r[0:SP, :] += dot_nt(n1, dth)
                dn1 = dot(tw1_r[...], dth)
                scaled, inverse = normal(both_x[:, e, :].astype(F32))
                vec[2:3, :] += total_of(dn1 * scaled)
                vec[3:4, :] += total_of(dn1)
                dacc[i] = du + norm_back(dn1, g1_r[...], scaled, inverse)

        def flush_pair(p):
            for e in range(2):
                gcopy(2 * p + e).start()

        def ocopy(i):
            return pltpu.make_async_copy(outs.at[i], out_h.at[i], o_sem.at[i])

        def flush_result(j):
            for e in range(2):
                ocopy(2 * j + e).start()

        def result(j):
            rr = chunk_at(j)
            total = dot(ca[0, rr, :], W2[t])
            for k in range(1, nt):
                total += dot(ca[k, rr, :], W2[order[k]])
            for e in range(2):
                v = total[e * SP : e * SP + S, :] * 0.5 + u_s[2 * j + e] + cb2_r[...]
                outs[2 * j + e] = v.astype(BF)

        for p in range(pairs):
            xcopy(p, p).start()
        act(3, 3)

        def final(j, carry):
            @pl.when(j == 1)
            def _():
                sum_step(2)

            last(j)
            return carry

        lax.fori_loop(0, n_chunk, final, 0)

        def token(p, carry):
            @pl.when(p == 1)
            def _():
                sum_step(3)


            token_back(p)
            flush_pair(p)
            return carry

        lax.fori_loop(0, pairs, token, 0)

        low = 2 * SP
        sm_r[SP : SP + S, :] = sm_r[SP : SP + S, :] * 0.5
        for k in range(5):
            for h in range(2):
                sm_r[low + 2 * k + h : low + 2 * k + h + 1, :] = vec[k : k + 1, h * HD : (h + 1) * HD]
        sm_r[low + 10 : low + 11, 0:S] = total_of(eye(S, F32) * tb2acc[...])
        for s in range(nt):
            for h in range(2):
                r = low + 11 + 2 * s + h
                sm_r[r : r + 1, :] = jnp.where(t == s, 1.0, 0.0) * gcb1[:, h * HD : (h + 1) * HD]

        part = SMALL // RING
        s_snd[...] = sm_r[...].astype(BF)

        def eighths(k, back):
            whom = (base + (l + k) % RING, t)
            if back:
                ref = s_all.at[pl.ds(pl.multiple_of(l * part, part), part)]
                return remote(ref, ref, sqs.at[k], sqr.at[k], whom)
            src = s_snd.at[pl.ds(pl.multiple_of(((l + k) % RING) * part, part), part)]
            return remote(src, s_rcv.at[k], sps.at[k], spr.at[k], whom)

        def across(k):
            return remote(z_rcv.at[t], z_rcv.at[t], szs.at[k], szr.at[k], (b, (t + k) % nt))

        for k in range(1, RING):
            eighths(k, False).start()

        def small_step(stage):
            if stage == 1:
                total = sm_r[pl.ds(pl.multiple_of(l * part, part), part), :]
                for k in range(1, RING):
                    eighths(k, False).wait()
                    total += s_rcv[k].astype(F32)
                z_rcv[t] = total.astype(BF)
                for k in range(1, nt):
                    across(k).start()
            elif stage == 2:
                for k in range(1, nt):
                    across(k).wait()
                total = z_rcv[0].astype(F32)
                for s in range(1, nt):
                    total += z_rcv[s].astype(F32)
                for n, e in enumerate(extra):
                    x_snd[n] = total.astype(BF)
                    cp = remote(x_snd.at[n], x_rcv.at[n], sxs.at[n], sxr.at[n], (flip(b, e), t))
                    cp.start()
                    cp.wait()
                    total = x_snd[n].astype(F32) + x_rcv[n].astype(F32)
                s_all[pl.ds(pl.multiple_of(l * part, part), part), :] = total.astype(BF)
                for k in range(1, RING):
                    eighths(k, True).start()
            else:
                for k in range(1, RING):
                    eighths(k, True).wait()

        def rest(j, carry):
            @pl.when(j == 0)
            def _():
                sum_step(4)

            @pl.when(j == 2)
            def _():
                small_step(1)

            result(j)
            flush_result(j)
            return carry

        lax.fori_loop(0, n_chunk, rest, 0)
        small_step(2)
        sum_step(5)
        sum_copy(5).wait()
        flush = pltpu.make_async_copy(gwb, gwb_o, l_sem.at[0])
        flush.start()
        for i in range(own):
            ocopy(i).wait()
            gcopy(i).wait()
        small_step(3)
        flush.wait()

    V = pltpu.VMEM
    DMA = pltpu.SemaphoreType.DMA
    any_ = pl.BlockSpec(memory_space=pl.ANY)
    vm = pl.BlockSpec(memory_space=V)
    f = lambda *shape: jax.ShapeDtypeStruct(shape, F32)
    h = lambda *shape: jax.ShapeDtypeStruct(shape, BF)
    xn = max(1, len(extra))
    part = SMALL // RING
    raw = pl.pallas_call(
        kernel,
        out_shape=(h(own, S, D), f(own, S, D), h(2, D, D), h(SMALL, DS)),
        in_specs=[any_, any_, any_, any_, vm, pl.BlockSpec(memory_space=pltpu.SMEM)] + [vm] * 9,
        out_specs=(any_, any_, any_, vm),
        scratch_shapes=[
            V((nt, D, H), BF), V((nt, H, D), BF), V((nt, 1, H), F32),
            V((SLOTS, S, 2, D), BF), V((SLOTS, S, 2, D), BF),
            V((rows, D), BF), V((rows, D), BF), V((rows, D), BF), V((rows, D), BF),
            V((nt, rows, H), BF), V((rows, H), BF), V((own, S, D), F32),
            V((own, S, D), F32), V((own, DS, D), BF), V((own, SP, D), BF),
            V((DS, S), BF), V((S, DS), BF), V((DS, S), BF), V((DS, 1), F32), V((S, 1), F32),
            V((1, H), F32), V((8, D), F32), V((S, 1), F32), V((own, S, D), BF),
            V((1, H), F32), V((1, D), F32), V((1, D), F32), V((1, D), F32), V((1, D), F32), V((1, D), F32),
            V((2, D, D), F32), V((SMALL, DS), F32),
            V((D, D), BF), V((D // 2, D), BF), V((D // 4, D), BF),
            V((xn, D // 4, D), BF), V((2, D, D), BF),
            V((SMALL, DS), BF), V((RING, part, DS), BF), V((nt, part, DS), BF),
            V((xn, part, DS), BF), V((xn, part, DS), BF),
            DMA((SLOTS,)), DMA((SLOTS,)), DMA((2,)), DMA((own,)), DMA((own,)),
            DMA((2, nt, 2)), DMA((2, nt, 2)), DMA((nt, 7, 2)), DMA((nt, 7, 2)), DMA((nt,)), DMA((nt,)),
            DMA((6,)), DMA((6,)), DMA((xn,)), DMA((xn,)), DMA((RING,)), DMA((RING,)), DMA((nt,)), DMA((nt,)),
            DMA((xn,)), DMA((xn,)), DMA((RING,)), DMA((RING,)),
        ],
        compiler_params=pltpu.CompilerParams(
            collective_id=0, has_side_effects=True, vmem_limit_bytes=65200 * 1024
        ),
    )(
        jnp.swapaxes(images, 0, 1), jnp.swapaxes(cot, 0, 1), cw1, cw2, cb1, counts,
        g1, b1, g2, b2, tw1, tw2.T, tb1, tb2, cb2,
    )

    def unpack(
        out_r, gim_r, gwb_r, s_all,
        out_o, gim_o, gg1_o, gb1_o, gtw1_o, gtb1_o, gtw2_o, gtb2_o, gg2_o, gb2_o, gw1_o, gcb1_o, gw2_o, gcb2_o,
        o_s, m_s, b_s, w_s, sem_in, sem,
    ):
        t = lax.axis_index("tensor")
        cuts = [(gwb_r.at[n], b_s.at[n]) for n in range(2)]
        cuts += [(gim_r.at[i], m_s.at[i]) for i in range(own)]
        cuts += [(out_r.at[i], o_s.at[i]) for i in range(own)]
        goals = [gw1_o, gw2_o] + [gim_o.at[i] for i in range(own)] + [out_o.at[i] for i in range(own)]
        loads = [pltpu.make_async_copy(src, dst, sem_in.at[n]) for n, (src, dst) in enumerate(cuts)]
        for cp in loads:
            cp.start()
        moves = []
        for n, ref in enumerate(goals):
            loads[n].wait()
            src = cuts[n][1]
            if n < 2:
                w_s[n] = b_s[n].astype(F32)
                src = w_s.at[n]
            moves.append(pltpu.make_async_copy(src, ref, sem.at[n]))
            moves[-1].start()
        low = 2 * SP
        gtw1_o[...] = s_all[0:S, :].astype(F32)
        gtw2_o[...] = s_all[SP : SP + S, :].astype(F32)
        ends = s_all[low : low + 32, :].astype(F32)
        at = S // 16 * 16
        gtb1_o[...] = s_all[at : at + 16, :].astype(F32)[S - at]
        gtb2_o[...] = ends[10, 0:S]
        for k, ref in enumerate((gg2_o, gb2_o, gg1_o, gb1_o, gcb2_o)):
            for h in range(2):
                ref[h * HD : (h + 1) * HD] = ends[2 * k + h]
        for h in range(2):
            total = ends[11 + h] * jnp.where(t == 0, 1.0, 0.0)
            for s in range(1, nt):
                total += ends[11 + 2 * s + h] * jnp.where(t == s, 1.0, 0.0)
            gcb1_o[h * HD : (h + 1) * HD] = total
        for cp in moves:
            cp.wait()

    out = pl.pallas_call(
        unpack,
        out_shape=(
            h(own, S, D), f(own, S, D), f(D), f(D), f(S, DS), f(DS), f(S, DS), f(S), f(D), f(D),
            f(D, H), f(H), f(H, D), f(D),
        ),
        in_specs=[any_, any_, any_, vm],
        out_specs=(any_, any_) + (vm,) * 8 + (any_, vm, any_, vm),
        scratch_shapes=[
            V((own, S, D), BF), V((own, S, D), F32), V((2, D, D), BF), V((2, D, D), F32),
            DMA((2 + 2 * own,)), DMA((2 + 2 * own,)),
        ],
        compiler_params=pltpu.CompilerParams(vmem_limit_bytes=65200 * 1024),
    )(*raw)
    return out[:6] + (out[6].T,) + out[7:]


def solution(mesh):
    nb, nt = mesh.shape["batch"], mesh.shape["tensor"]
    in_specs = (
        P("batch", None, None), P("batch"),
        P(), P(), P(), P(), P(), P(), P(), P(),
        P(None, "tensor"), P("tensor"), P("tensor", None), P(),
        P("batch", None, None),
    )
    both = P(("batch", "tensor"), None, None)
    out_specs = (
        both, both,
        P(), P(), P(), P(), P(), P(), P(), P(),
        P(None, "tensor"), P("tensor"), P("tensor", None), P(),
    )
    return jax.shard_map(
        lambda *args: per_device(nb, nt, args),
        mesh=mesh, in_specs=in_specs, out_specs=out_specs, check_vma=False,
    )
```
